768 devices in a mesh: seq: 192 (over y, x_hi, z), tp: 4 (over x_lo, core).
Axes of the slice: x: 4 (x_hi: 2, x_lo: 2; x = x_hi * 2 + x_lo), y: 8, z: 12, core: 2. Of those that a mesh axis runs over, the one named last changes fastest.
Arguments:
- hidden: bfloat16 [49152, 4096], P('seq', 'tp'), may hold values from -6 to 6
- in_proj: bfloat16 [4096, 1024], P('tp'), may hold values from -0.09375 to 0.09375
- norm_gain: float32 [1024], replicated, may hold values from 0.25 to 1.75
- head_weight: bfloat16 [1024, 2048], P(None, 'tp'), may hold values from -0.625 to 0.625
- code_ids: int32 [49152], P('seq'), may hold values from 0 to 2047
- stream_mask: int32 [49152], P('seq'), may hold values from 0 to 1
Outputs:
- hidden_grad: bfloat16 [49152, 4096], P('seq', 'tp')
- weight_grads: float32 [4, 3072, 512], P('tp', 'seq')
The draws below stay inside these ranges and needn't reach their ends.
All inputs are finite; a program needn't handle non-finite values.
Results may differ from the reference program's by a relative error of at most 0.029.
Values may be sent and summed in bfloat16 or wider, within the bound.
No kernel may reach another device: no remote copies, remote signals or barrier semaphores. Data moves between devices by JAX's collectives and lax.ppermute only.
A program may use at most 64 MiB of HBM per device.

```python
import jax
import jax.numpy as jnp
from jax import lax

D = 4096
W = 1024
V = 2048
FRAMES = 49152
VS = 512
N_TP = 4


def draw_stream_mask(key, part):
    positions = jnp.arange(FRAMES, dtype=jnp.int32)
    tickets = jax.random.randint(key, (FRAMES,), 0, 4 * FRAMES, dtype=jnp.int32)
    return jnp.where(tickets < FRAMES + 2 * positions, 1, 0).astype(jnp.int32)


def with_ends(array, stream_key, smallest, largest):
    place = [jax.random.randint(jax.random.fold_in(stream_key, axis), (), 0, length) for axis, length in enumerate(array.shape)]
    main_axis = array.shape.index(max(array.shape))
    next_to = place[:main_axis] + [(place[main_axis] + 1) % array.shape[main_axis]] + place[main_axis + 1:]
    return array.at[tuple(place)].set(smallest).at[tuple(next_to)].set(largest)


def block_levels(rng, extent, cuts, smallest, top_value):
    gain, own = 1.0, jax.random.fold_in(rng, 6)
    for dim, shards_of in cuts:
        draws = jnp.exp(jax.random.uniform(jax.random.fold_in(own, dim), (shards_of,), jnp.float32, smallest / len(cuts), top_value / len(cuts)))
        gain = gain * jnp.repeat(draws, extent[dim] // shards_of).reshape([-1 if axis == dim else 1 for axis in range(len(extent))])
    return gain


def centred(stream_key, dims, scale, limit, pieces=(), kind=jnp.bfloat16):
    entries = jax.random.normal(stream_key, dims, jnp.float32) * scale
    if len(pieces) > 0:
        entries = block_levels(stream_key, dims, pieces, -0.22, 0.18) * entries
    return jnp.clip(entries, min=-limit, max=limit).astype(kind)


def setup_inputs(seed: int = 0) -> dict:
    seeds = jax.random.split(jax.random.key(seed), 7)
    return {
        "hidden": centred(seeds[0], (FRAMES, D), 1.0, 6.0, ((0, 192), (1, 4))),
        "in_proj": centred(seeds[1], (D, W), D ** -0.5, 0.09375, ((0, 4),)),
        "norm_gain": jnp.clip(1.0 + 0.15 * jax.random.normal(seeds[2], (W,), jnp.float32), 0.25, 1.75),
        "head_weight": centred(seeds[3], (W, V), 0.1, 0.625, ((1, 4),)),
        "code_ids": with_ends(jax.random.randint(seeds[4], (FRAMES,), 0, V), jax.random.fold_in(seeds[4], 1), 0, V - 1).astype(jnp.int32),
        "stream_mask": draw_stream_mask(jax.random.fold_in(seeds[6], 71), 0),
    }


norm_eps = 1e-05
loss_scale = 16.0

def reference(hidden, in_proj, norm_gain, head_weight, code_ids, stream_mask):
    projected = jnp.dot(hidden, in_proj, preferred_element_type=jnp.float32)
    inv_rms = lax.rsqrt(lax.optimization_barrier(jnp.mean(projected * projected, axis=1, keepdims=True)) + norm_eps)
    unit_rows = projected * inv_rms
    normed = (unit_rows * norm_gain[None, :]).astype(jnp.bfloat16)
    logits = jnp.dot(normed, head_weight, preferred_element_type=jnp.float32)
    exp_logits = jnp.exp(logits)
    exp_total = lax.optimization_barrier(jnp.sum(exp_logits, axis=1, keepdims=True))
    columns = lax.broadcasted_iota(jnp.int32, logits.shape, 1)
    onehot = (columns == code_ids[:, None].astype(jnp.int32)).astype(jnp.float32)
    weighting = stream_mask.astype(jnp.float32)[:, None]
    dlogit = (weighting * (exp_logits / exp_total - onehot)).astype(jnp.bfloat16)
    normed_grad = lax.dot_general(dlogit, head_weight, (((1,), (1,)), ((), ())), preferred_element_type=jnp.float32)
    scaled_grad = normed_grad * norm_gain[None, :]
    row_grad = (inv_rms * (scaled_grad - unit_rows * lax.optimization_barrier(jnp.mean(scaled_grad * unit_rows, axis=1, keepdims=True)))).astype(jnp.bfloat16)
    hidden_grad = (loss_scale * lax.dot_general(row_grad, in_proj, (((1,), (1,)), ((), ())), preferred_element_type=jnp.float32)).astype(jnp.bfloat16)
    head_grad = lax.dot_general(normed, dlogit, (((0,), (0,)), ((), ())), preferred_element_type=jnp.float32)
    proj_grad = lax.dot_general(hidden, row_grad, (((0,), (0,)), ((), ())), preferred_element_type=jnp.float32)
    proj_part = proj_grad.reshape(N_TP, D // N_TP * W // VS, VS)
    head_part = jnp.transpose(head_grad.reshape(W, N_TP, VS), (1, 0, 2))
    weight_grads = jnp.concatenate([proj_part, head_part], axis=1)
    return (hidden_grad, weight_grads)
```

```python
import jax
import jax.numpy as jnp
from jax import lax
from jax.sharding import Mesh
from jax.sharding import PartitionSpec as P

norm_eps = 1e-05
loss_scale = 16.0

AXES = ("yh", "yl", "xh", "zh", "zl", "xl", "core")
SIZES = (4, 2, 2, 6, 2, 2, 2)
SEQ = ("yh", "yl", "xh", "zh", "zl")
TP = ("xl", "core")
NEAR = ("yl", "xh", "zl")
FAR = ("yh", "zh")
N_TP = 4
N_NEAR = 8
N_FAR = 24
BLOCKS = 192
PROJ_BLOCKS = 128
f32 = jnp.float32
bf16 = jnp.bfloat16


def dot(a, b, ca, cb):
    return lax.dot_general(a, b, (((ca,), (cb,)), ((), ())), preferred_element_type=f32)


def local(hidden, in_proj, norm_gain, head_weight, code_ids, stream_mask):
    frames, width = hidden.shape[0], in_proj.shape[1]
    vocab_part = head_weight.shape[1]
    own = frames // N_TP
    tp = lax.axis_index(TP)
    gain = norm_gain[None, :]

    partial_x = dot(hidden, in_proj, 1, 0).astype(bf16)
    pieces = lax.all_to_all(partial_x.reshape(N_TP, own, width), TP, 0, 0)
    x = jnp.sum(pieces.astype(f32), axis=0)
    inv_rms = lax.rsqrt(jnp.mean(x * x, axis=1, keepdims=True) + norm_eps)
    unit_rows = x * inv_rms
    normed = lax.all_gather((unit_rows * gain).astype(bf16), TP, tiled=True)

    exp_logits = jnp.exp(dot(normed, head_weight, 1, 0))
    totals = lax.all_gather(jnp.sum(exp_logits, axis=1), TP)
    exp_total = jnp.sum(totals, axis=0)[:, None]
    columns = lax.broadcasted_iota(jnp.int32, (frames, vocab_part), 1) + tp * vocab_part
    onehot = (columns == code_ids[:, None]).astype(f32)
    weighting = stream_mask.astype(f32)[:, None]
    dlogit = (weighting * (exp_logits / exp_total - onehot)).astype(bf16)

    partial_grad = dot(dlogit, head_weight, 1, 1).astype(bf16)
    pieces = lax.all_to_all(partial_grad.reshape(N_TP, own, width), TP, 0, 0)
    head_grad = dot(normed, dlogit, 0, 0).astype(bf16)
    scaled_grad = jnp.sum(pieces.astype(f32), axis=0) * gain
    centred = scaled_grad - unit_rows * jnp.mean(scaled_grad * unit_rows, axis=1, keepdims=True)
    own_grad = (inv_rms * centred).astype(bf16)
    row_grad = lax.all_to_all(
        jnp.broadcast_to(own_grad[None], (N_TP, own, width)), TP, 0, 0
    ).reshape(frames, width)

    proj_grad = dot(hidden, row_grad, 0, 0).astype(bf16)
    proj_blocks = proj_grad.reshape(PROJ_BLOCKS, 8, width)
    head_blocks = head_grad.reshape(BLOCKS - PROJ_BLOCKS, 2, 8, vocab_part)
    head_blocks = jnp.transpose(head_blocks, (0, 2, 1, 3)).reshape(BLOCKS - PROJ_BLOCKS, 8, width)
    blocks = jnp.concatenate([proj_blocks, head_blocks], axis=0)
    blocks = blocks.reshape(4, 2, 2, 6, 2, 8, width)
    blocks = jnp.transpose(blocks, (1, 2, 4, 0, 3, 5, 6)).reshape(N_NEAR, N_FAR * 8, width)
    near = lax.all_to_all(blocks, NEAR, 0, 0)
    near = jnp.sum(near.astype(f32), axis=0).astype(bf16).reshape(N_FAR, 8, width)
    far = lax.all_to_all(near, FAR, 0, 0)
    summed = jnp.sum(far.astype(f32), axis=0)
    as_proj = summed.reshape(16, vocab_part)
    as_head = jnp.concatenate([summed[:, :vocab_part], summed[:, vocab_part:]], axis=0)
    weight_grads = jnp.where(lax.axis_index(SEQ) < PROJ_BLOCKS, as_proj, as_head)

    hidden_grad = (loss_scale * dot(row_grad, in_proj, 1, 1)).astype(bf16)
    return (hidden_grad, weight_grads[None])


def solution(mesh):
    fine = Mesh(mesh.devices.reshape(SIZES), AXES)
    in_specs = (P(SEQ, TP), P(TP, None), P(), P(None, TP), P(SEQ), P(SEQ))
    out_specs = (P(SEQ, TP), P(TP, SEQ, None))
    return jax.shard_map(local, mesh=fine, in_specs=in_specs, out_specs=out_specs, check_vma=False)
```

```python
import jax
import jax.numpy as jnp
from jax import lax
from jax.sharding import Mesh
from jax.sharding import PartitionSpec as P

norm_eps = 1e-05
loss_scale = 16.0

AXES = ("yh", "yl", "xh", "zh", "zl", "xl", "core")
SIZES = (4, 2, 2, 6, 2, 2, 2)
SEQ = ("yh", "yl", "xh", "zh", "zl")
TP = ("xl", "core")
NEAR = ("yl", "xh", "zl")
N_TP = 4
N_NEAR = 8
BLOCKS = 192
PROJ_BLOCKS = 128
f32 = jnp.float32
bf16 = jnp.bfloat16


def dot(a, b, ca, cb):
    return lax.dot_general(a, b, (((ca,), (cb,)), ((), ())), preferred_element_type=f32)


def add_up(pieces):
    total = pieces[0].astype(f32)
    for i in range(1, pieces.shape[0]):
        total = total + pieces[i].astype(f32)
    return total


def near_sum(blocks, n_yh):
    blocks = blocks.reshape(n_yh, 2, 2, 6, 2, 8, blocks.shape[-1])
    blocks = jnp.transpose(blocks, (1, 2, 4, 0, 3, 5, 6)).reshape(N_NEAR, n_yh * 6 * 8, -1)
    near = add_up(lax.all_to_all(blocks, NEAR, 0, 0)).astype(bf16)
    return near.reshape(n_yh, 6, 8, near.shape[-1])


def local(hidden, in_proj, norm_gain, head_weight, code_ids, stream_mask):
    frames, width = hidden.shape[0], in_proj.shape[1]
    vocab_part = head_weight.shape[1]
    own = frames // N_TP
    tp = lax.axis_index(TP)
    gain = norm_gain[None, :]

    partial_x = dot(hidden, in_proj, 1, 0).astype(bf16)
    x = add_up(lax.all_to_all(partial_x.reshape(N_TP, own, width), TP, 0, 0))
    inv_rms = lax.rsqrt(jnp.mean(x * x, axis=1, keepdims=True) + norm_eps)
    unit_rows = x * inv_rms
    normed = lax.all_gather((unit_rows * gain).astype(bf16), TP, tiled=True)

    exp_logits = jnp.exp(dot(normed, head_weight, 1, 0))
    totals = lax.all_gather(jnp.sum(exp_logits, axis=1), TP)
    exp_total = jnp.sum(totals, axis=0)[:, None]
    columns = lax.broadcasted_iota(jnp.int32, (frames, vocab_part), 1) + tp * vocab_part
    onehot = (columns == code_ids[:, None]).astype(f32)
    weighting = stream_mask.astype(f32)[:, None]
    dlogit = (weighting * (exp_logits / exp_total - onehot)).astype(bf16)

    partial_grad = dot(dlogit, head_weight, 1, 1).astype(bf16)
    pieces = lax.all_to_all(partial_grad.reshape(N_TP, own, width), TP, 0, 0)

    head_grad = dot(normed, dlogit, 0, 0).astype(bf16)
    head_blocks = head_grad.reshape(BLOCKS - PROJ_BLOCKS, 2, 8, vocab_part)
    head_blocks = jnp.transpose(head_blocks, (0, 2, 1, 3)).reshape(BLOCKS - PROJ_BLOCKS, 8, width)
    head_blocks = jnp.pad(head_blocks, ((PROJ_BLOCKS - 96, 0), (0, 0), (0, 0)))
    head_near = near_sum(head_blocks, 2)

    scaled_grad = add_up(pieces) * gain
    centred = scaled_grad - unit_rows * jnp.mean(scaled_grad * unit_rows, axis=1, keepdims=True)
    row_grad = lax.all_gather((inv_rms * centred).astype(bf16), TP, tiled=True)

    proj_grad = dot(hidden, row_grad, 0, 0).astype(bf16)
    proj_blocks = jnp.pad(proj_grad.reshape(PROJ_BLOCKS, 8, width), ((0, 144 - PROJ_BLOCKS), (0, 0), (0, 0)))
    proj_near = near_sum(proj_blocks, 3)
    hidden_grad = (loss_scale * dot(row_grad, in_proj, 1, 1)).astype(bf16)

    near_place = (lax.axis_index("yl") * 2 + lax.axis_index("xh")) * 12 + lax.axis_index("zl")
    mixed = 96 + near_place + 2 * jnp.arange(6)
    third = jnp.where((mixed < PROJ_BLOCKS)[:, None, None], proj_near[2], head_near[0])
    near = jnp.concatenate([proj_near[:2], third[None], head_near[1:]], axis=0)
    far = add_up(lax.all_to_all(near, "yh", 0, 0)).astype(bf16)
    summed = add_up(lax.all_to_all(far, "zh", 0, 0))
    block = lax.axis_index(SEQ)
    as_proj = summed.reshape(16, vocab_part)
    as_head = jnp.concatenate([summed[:, :vocab_part], summed[:, vocab_part:]], axis=0)
    weight_grads = jnp.where(block < PROJ_BLOCKS, as_proj, as_head)
    return (hidden_grad, weight_grads[None])


def solution(mesh):
    fine = Mesh(mesh.devices.reshape(SIZES), AXES)
    in_specs = (P(SEQ, TP), P(TP, None), P(), P(None, TP), P(SEQ), P(SEQ))
    out_specs = (P(SEQ, TP), P(TP, SEQ, None))
    return jax.shard_map(local, mesh=fine, in_specs=in_specs, out_specs=out_specs, check_vma=False)
```

```python
import jax
import jax.numpy as jnp
from jax import lax
from jax.sharding import Mesh
from jax.sharding import PartitionSpec as P

norm_eps = 1e-05
loss_scale = 16.0

AXES = ("yh", "yl", "xh", "zh", "zl", "xl", "core")
SIZES = (4, 2, 2, 6, 2, 2, 2)
SEQ = ("yh", "yl", "xh", "zh", "zl")
TP = ("xl", "core")
BLOCKS = 192
PROJ_BLOCKS = 128
HALF = 96
SWAP = [(0, 1), (1, 0)]
f32 = jnp.float32
bf16 = jnp.bfloat16


def dot(a, b, ca, cb):
    return lax.dot_general(a, b, (((ca,), (cb,)), ((), ())), preferred_element_type=f32)


def add_up(pieces):
    total = pieces[0].astype(f32)
    for i in range(1, pieces.shape[0]):
        total = total + pieces[i].astype(f32)
    return total


def tp_sum(partial):
    rows, width = partial.shape
    chip = add_up(lax.all_to_all(partial.reshape(2, rows // 2, width), "core", 0, 0)).astype(bf16)
    return add_up(lax.all_gather(chip, "xl"))


def halve(blocks, axis_name, axis):
    me = lax.axis_index(axis_name)
    sent = lax.dynamic_index_in_dim(blocks, 1 - me, axis, keepdims=False)
    kept = lax.dynamic_index_in_dim(blocks, me, axis, keepdims=False)
    return (kept.astype(f32) + lax.ppermute(sent, axis_name, SWAP).astype(f32)).astype(bf16)


def local(hidden, in_proj, norm_gain, head_weight, code_ids, stream_mask):
    frames, width = hidden.shape[0], in_proj.shape[1]
    vocab_part = head_weight.shape[1]
    tp = lax.axis_index(TP)
    gain = norm_gain[None, :]

    x = tp_sum(dot(hidden, in_proj, 1, 0).astype(bf16))
    inv_rms = lax.rsqrt(jnp.mean(x * x, axis=1, keepdims=True) + norm_eps)
    unit_rows = x * inv_rms
    normed = lax.all_gather((unit_rows * gain).astype(bf16), "core", tiled=True)

    exp_logits = jnp.exp(dot(normed, head_weight, 1, 0))
    totals = lax.all_gather(jnp.sum(exp_logits, axis=1), TP)
    exp_total = jnp.sum(totals, axis=0)[:, None]
    columns = lax.broadcasted_iota(jnp.int32, (frames, vocab_part), 1) + tp * vocab_part
    onehot = (columns == code_ids[:, None]).astype(f32)
    weighting = stream_mask.astype(f32)[:, None]
    dlogit = (weighting * (exp_logits / exp_total - onehot)).astype(bf16)

    scaled_grad = tp_sum(dot(dlogit, head_weight, 1, 1).astype(bf16)) * gain
    head_grad = dot(normed, dlogit, 0, 0).astype(bf16)
    head_blocks = head_grad.reshape(BLOCKS - PROJ_BLOCKS, 2, 8, vocab_part)
    head_blocks = jnp.transpose(head_blocks, (0, 2, 1, 3)).reshape(BLOCKS - PROJ_BLOCKS, 8, width)

    centred = scaled_grad - unit_rows * jnp.mean(scaled_grad * unit_rows, axis=1, keepdims=True)
    row_grad = lax.all_gather((inv_rms * centred).astype(bf16), "core", tiled=True)

    split = HALF * 8
    late = dot(hidden[:, split:], row_grad, 0, 0).astype(bf16).reshape(PROJ_BLOCKS - HALF, 8, width)
    early = dot(hidden[:, :split], row_grad, 0, 0).astype(bf16)
    shape = (2, 2, 2, 6, 2, 8, width)
    late = jnp.concatenate([late, head_blocks], axis=0).reshape(shape)
    early = early.reshape(shape)
    late = halve(late, "yl", 1)
    early = halve(early, "zl", 4)
    late = halve(late, "zl", 3)
    early = halve(early, "yl", 1)
    near = jnp.concatenate([early, late], axis=0).reshape(8, 6 * 8, width)
    mid = add_up(lax.all_to_all(near, ("yh", "xh"), 0, 0)).astype(bf16).reshape(6, 8, width)
    summed = add_up(lax.all_to_all(mid, "zh", 0, 0))
    as_proj = summed.reshape(16, vocab_part)
    as_head = jnp.concatenate([summed[:, :vocab_part], summed[:, vocab_part:]], axis=0)
    weight_grads = jnp.where(lax.axis_index(SEQ) < PROJ_BLOCKS, as_proj, as_head)

    hidden_grad = (loss_scale * dot(row_grad, in_proj, 1, 1)).astype(bf16)
    return (hidden_grad, weight_grads[None])


def solution(mesh):
    fine = Mesh(mesh.devices.reshape(SIZES), AXES)
    in_specs = (P(SEQ, TP), P(TP, None), P(), P(None, TP), P(SEQ), P(SEQ))
    out_specs = (P(SEQ, TP), P(TP, SEQ, None))
    return jax.shard_map(local, mesh=fine, in_specs=in_specs, out_specs=out_specs, check_vma=False)
```

```python
import jax
import jax.numpy as jnp
from jax import lax
from jax.experimental import pallas as pl
from jax.experimental.pallas import tpu as pltpu
from jax.sharding import Mesh
from jax.sharding import PartitionSpec as P

norm_eps = 1e-05
loss_scale = 16.0

AXES = ("yh", "yl", "xh", "zh", "zl", "xl", "core")
SIZES = (4, 2, 2, 6, 2, 2, 2)
SEQ = ("yh", "yl", "xh", "zh", "zl")
TP = ("xl", "core")
NEAR = ("yl", "xh", "zl")
FAR = ("yh", "zh")
N_NEAR = 8
N_FAR = 24
BLOCKS = 192
PROJ_BLOCKS = 128
VMEM_BYTES = 20 << 20
SWAP = [(0, 1), (1, 0)]
f32 = jnp.float32
bf16 = jnp.bfloat16


def dot(a, b, ca, cb):
    return lax.dot_general(a, b, (((ca,), (cb,)), ((), ())), preferred_element_type=f32)


def add_up(pieces):
    total = pieces[0].astype(f32)
    for i in range(1, pieces.shape[0]):
        total = total + pieces[i].astype(f32)
    return total


def near_far(block):
    y, x, z = block // 24, block // 12 % 2, block % 12
    return (y % 2 * 2 + x) * 2 + z % 2, y // 2 * 6 + z // 2


def rows_product(half_ref, a_ref, b_ref, out_ref):
    rows = out_ref.shape[0]
    start = pl.multiple_of(half_ref[0] * rows, rows)
    out_ref[...] = dot(a_ref[pl.ds(start, rows), :], b_ref[...], 1, 0).astype(out_ref.dtype)


def exp_rows(normed_ref, head_ref, exp_ref, sum_ref):
    exp_logits = jnp.exp(dot(normed_ref[...], head_ref[...], 1, 0))
    exp_ref[...] = exp_logits
    sum_ref[...] = jnp.sum(exp_logits, axis=1, keepdims=True)


def dlogit_rows(first, exp_ref, totals_ref, code_ref, mask_ref, rows):
    window = pl.ds(first, rows)
    exp_logits = exp_ref[window, :]
    columns = lax.broadcasted_iota(jnp.int32, exp_logits.shape, 1)
    onehot = (columns == code_ref[window, :]).astype(f32)
    return (mask_ref[window, :] * (exp_logits / totals_ref[window, :] - onehot)).astype(bf16)


def sent_grad(half_ref, exp_ref, totals_ref, code_ref, mask_ref, head_ref, out_ref):
    rows = out_ref.shape[0]
    start = pl.multiple_of(half_ref[0] * rows, rows)
    dlogit = dlogit_rows(start, exp_ref, totals_ref, code_ref, mask_ref, rows)
    out_ref[...] = dot(dlogit, head_ref[...], 1, 1).astype(out_ref.dtype)


def kept_grad(half_ref, exp_ref, totals_ref, code_ref, mask_ref, head_ref, normed_ref, out_ref, blocks_ref):
    rows = out_ref.shape[0]
    start = pl.multiple_of(half_ref[0] * rows, rows)
    dlogit = dlogit_rows(start, exp_ref, totals_ref, code_ref, mask_ref, rows)
    out_ref[...] = dot(dlogit, head_ref[...], 1, 1)
    whole = dlogit_rows(0, exp_ref, totals_ref, code_ref, mask_ref, exp_ref.shape[0])
    grad = dot(normed_ref[...], whole, 0, 0).astype(bf16)
    part = grad.shape[1]
    for i in range(blocks_ref.shape[0]):
        blocks_ref[i, :, :part] = grad[16 * i : 16 * i + 8]
        blocks_ref[i, :, part:] = grad[16 * i + 8 : 16 * i + 16]


def grad_blocks(hidden_ref, grad_ref, head_ref, out_ref):
    step = 16
    for first in range(0, PROJ_BLOCKS, step):
        part = dot(hidden_ref[:, 8 * first : 8 * (first + step)], grad_ref[...], 0, 0).astype(bf16)
        for i in range(step):
            near, far = near_far(first + i)
            out_ref[near, 8 * far : 8 * far + 8, :] = part[8 * i : 8 * i + 8]
    for block in range(PROJ_BLOCKS, BLOCKS):
        near, far = near_far(block)
        out_ref[near, 8 * far : 8 * far + 8, :] = head_ref[block - PROJ_BLOCKS]


def near_sum(pieces_ref, out_ref):
    out_ref[...] = add_up(pieces_ref).astype(out_ref.dtype)


def far_sum(is_proj_ref, pieces_ref, out_ref):
    total = add_up(pieces_ref)
    part = out_ref.shape[2]
    left, right = total[:, :part], total[:, part:]

    @pl.when(is_proj_ref[0] == 1)
    def _():
        out_ref[:, 0, :] = left
        out_ref[:, 1, :] = right

    @pl.when(is_proj_ref[0] == 0)
    def _():
        for row in range(4):
            out_ref[row] = left[2 * row : 2 * row + 2]
            out_ref[4 + row] = right[2 * row : 2 * row + 2]


def in_vmem(kernel, outs, n_in, scalars=0):
    vmem = pl.BlockSpec(memory_space=pltpu.VMEM)
    smem = pl.BlockSpec(memory_space=pltpu.SMEM)
    return pl.pallas_call(
        kernel,
        out_shape=outs,
        in_specs=[smem] * scalars + [vmem] * n_in,
        out_specs=jax.tree.map(lambda _: vmem, outs),
        compiler_params=pltpu.CompilerParams(vmem_limit_bytes=VMEM_BYTES),
    )


def shape(dims, dtype):
    return jax.ShapeDtypeStruct(dims, dtype)


def local(hidden, in_proj, norm_gain, head_weight, code_ids, stream_mask):
    frames, width = hidden.shape[0], in_proj.shape[1]
    vocab_part = head_weight.shape[1]
    half = frames // 2
    tp = lax.axis_index(TP)
    gain = norm_gain[None, :]
    mine = lax.axis_index("core").reshape(1)
    other = 1 - mine
    code = (code_ids - tp * vocab_part)[:, None]
    mask = stream_mask.astype(f32)[:, None]

    def tp_sum(sent, kept):
        chip = (kept + lax.ppermute(sent, "core", SWAP).astype(f32)).astype(bf16)
        return add_up(lax.all_gather(chip, "xl"))

    sent = in_vmem(rows_product, shape((half, width), bf16), 2, 1)(other, hidden, in_proj)
    kept = in_vmem(rows_product, shape((half, width), f32), 2, 1)(mine, hidden, in_proj)
    x = tp_sum(sent, kept)
    inv_rms = lax.rsqrt(jnp.mean(x * x, axis=1, keepdims=True) + norm_eps)
    unit_rows = x * inv_rms
    normed = lax.all_gather((unit_rows * gain).astype(bf16), "core", tiled=True)

    exp_logits, sums = in_vmem(
        exp_rows, [shape((frames, vocab_part), f32), shape((frames, 1), f32)], 2
    )(normed, head_weight)
    exp_total = jnp.sum(lax.all_gather(sums[:, 0], TP), axis=0)[:, None]

    rest = (exp_logits, exp_total, code, mask, head_weight)
    sent = in_vmem(sent_grad, shape((half, width), bf16), 5, 1)(other, *rest)
    kept, head_blocks = in_vmem(
        kept_grad,
        [shape((half, width), f32), shape((BLOCKS - PROJ_BLOCKS, 8, width), bf16)],
        6,
        1,
    )(mine, *rest, normed)
    scaled_grad = tp_sum(sent, kept) * gain
    centred = scaled_grad - unit_rows * jnp.mean(scaled_grad * unit_rows, axis=1, keepdims=True)
    row_grad = lax.all_gather((inv_rms * centred).astype(bf16), "core", tiled=True)

    blocks = in_vmem(grad_blocks, shape((N_NEAR, N_FAR * 8, width), bf16), 3)(hidden, row_grad, head_blocks)
    pieces = lax.all_to_all(blocks, NEAR, 0, 0)
    rows = 32
    near = pl.pallas_call(
        near_sum,
        out_shape=shape((N_FAR * 8, width), bf16),
        grid=(N_FAR * 8 // rows,),
        in_specs=[pl.BlockSpec((N_NEAR, rows, width), lambda i: (0, i, 0))],
        out_specs=pl.BlockSpec((rows, width), lambda i: (i, 0)),
        compiler_params=pltpu.CompilerParams(vmem_limit_bytes=VMEM_BYTES),
    )(pieces)
    far = lax.all_to_all(near.reshape(N_FAR, 8, width), FAR, 0, 0)
    is_proj = (lax.axis_index(SEQ) < PROJ_BLOCKS).astype(jnp.int32).reshape(1)
    weight_grads = in_vmem(far_sum, shape((8, 2, vocab_part), f32), 1, 1)(is_proj, far).reshape(16, vocab_part)

    hidden_grad = (loss_scale * dot(row_grad, in_proj, 1, 1)).astype(bf16)
    return (hidden_grad, weight_grads[None])


def solution(mesh):
    fine = Mesh(mesh.devices.reshape(SIZES), AXES)
    in_specs = (P(SEQ, TP), P(TP, None), P(), P(None, TP), P(SEQ), P(SEQ))
    out_specs = (P(SEQ, TP), P(TP, SEQ, None))
    return jax.shard_map(local, mesh=fine, in_specs=in_specs, out_specs=out_specs, check_vma=False)
```

```python
import jax
import jax.numpy as jnp
from jax import lax
from jax.experimental import pallas as pl
from jax.experimental.pallas import tpu as pltpu
from jax.sharding import Mesh
from jax.sharding import PartitionSpec as P

norm_eps = 1e-05
loss_scale = 16.0

AXES = ("yh", "yl", "xh", "zh", "zl", "xl", "core")
SIZES = (4, 2, 2, 6, 2, 2, 2)
SEQ = ("yh", "yl", "xh", "zh", "zl")
TP = ("xl", "core")
NEAR = ("yl", "xh", "zl")
FAR = ("yh", "zh")
N_NEAR = 8
N_FAR = 24
BLOCKS = 192
PROJ_BLOCKS = 128
VMEM_BYTES = 20 << 20
SWAP = [(0, 1), (1, 0)]
f32 = jnp.float32
bf16 = jnp.bfloat16


def dot(a, b, ca, cb):
    return lax.dot_general(a, b, (((ca,), (cb,)), ((), ())), preferred_element_type=f32)


def add_up(pieces):
    total = pieces[0].astype(f32)
    for i in range(1, pieces.shape[0]):
        total = total + pieces[i].astype(f32)
    return total


def near_far(block):
    y, x, z = block // 24, block // 12 % 2, block % 12
    return (y % 2 * 2 + x) * 2 + z % 2, y // 2 * 6 + z // 2


def rows_product_sum(half_ref, a_ref, b_ref, other_ref, out_ref):
    rows = out_ref.shape[0]
    start = pl.multiple_of(half_ref[0] * rows, rows)
    kept = dot(a_ref[pl.ds(start, rows), :], b_ref[...], 1, 0)
    out_ref[...] = (kept + other_ref[...].astype(f32)).astype(out_ref.dtype)


def streamed_product(half_ref, a_hbm, b_hbm, out_ref, a_ref, b_ref, sems):
    rows, steps = out_ref.shape[0], b_ref.shape[0]
    start = pl.multiple_of(half_ref[0] * rows, rows)
    depth = b_ref.shape[1]
    copies = [pltpu.make_async_copy(a_hbm.at[pl.ds(start, rows), :], a_ref, sems.at[steps])]
    for i in range(steps):
        copies.append(pltpu.make_async_copy(b_hbm.at[i * depth : (i + 1) * depth, :], b_ref.at[i], sems.at[i]))
    for copy in copies:
        copy.start()
    copies[0].wait()
    total = None
    for i in range(steps):
        copies[1 + i].wait()
        part = dot(a_ref[:, i * depth : (i + 1) * depth], b_ref[i], 1, 0)
        total = part if total is None else total + part
    out_ref[...] = total.astype(out_ref.dtype)


def hidden_rows(grad_ref, b_hbm, out_ref, b_ref, sems):
    steps, depth = b_ref.shape[0], b_ref.shape[1]
    copies = [
        pltpu.make_async_copy(b_hbm.at[i * depth : (i + 1) * depth, :], b_ref.at[i], sems.at[i]) for i in range(steps)
    ]
    for copy in copies:
        copy.start()
    for i in range(steps):
        copies[i].wait()
        part = loss_scale * dot(grad_ref[...], b_ref[i], 1, 1)
        out_ref[:, i * depth : (i + 1) * depth] = part.astype(out_ref.dtype)


def exp_rows(normed_ref, head_ref, exp_ref, sum_ref):
    exp_logits = jnp.exp(dot(normed_ref[...], head_ref[...], 1, 0))
    exp_ref[...] = exp_logits
    ones = jnp.ones((8, exp_logits.shape[1]), f32)
    sums = lax.dot_general(
        ones, exp_logits, (((1,), (1,)), ((), ())), precision=lax.Precision.HIGHEST, preferred_element_type=f32
    )
    sum_ref[...] = sums[:1]


def spread(rows):
    ones = jnp.ones((rows.shape[0], 128), f32)
    return lax.dot_general(
        rows, ones, (((0,), (0,)), ((), ())), precision=lax.Precision.HIGHEST, preferred_element_type=f32
    )


def dlogit_rows(first, exp_ref, totals_ref, code_ref, mask_ref, rows):
    window = pl.ds(first, rows)
    total, code, mask = (spread(ref[:, window]) for ref in (totals_ref, code_ref, mask_ref))
    parts = []
    for start in range(0, exp_ref.shape[1], 128):
        columns = (lax.broadcasted_iota(jnp.int32, (rows, 128), 1) + start).astype(f32)
        onehot = (columns == code).astype(f32)
        parts.append((mask * (exp_ref[window, start : start + 128] / total - onehot)).astype(bf16))
    return jnp.concatenate(parts, axis=1)


def sent_grad(half_ref, exp_ref, totals_ref, code_ref, mask_ref, head_ref, out_ref):
    rows = out_ref.shape[0]
    start = pl.multiple_of(half_ref[0] * rows, rows)
    dlogit = dlogit_rows(start, exp_ref, totals_ref, code_ref, mask_ref, rows)
    out_ref[...] = dot(dlogit, head_ref[...], 1, 1).astype(out_ref.dtype)


def kept_grad(half_ref, exp_ref, totals_ref, code_ref, mask_ref, head_ref, normed_ref, out_ref, blocks_ref):
    rows = out_ref.shape[0]
    start = pl.multiple_of(half_ref[0] * rows, rows)
    dlogit = dlogit_rows(start, exp_ref, totals_ref, code_ref, mask_ref, rows)
    out_ref[...] = dot(dlogit, head_ref[...], 1, 1)
    whole = dlogit_rows(0, exp_ref, totals_ref, code_ref, mask_ref, exp_ref.shape[0])
    grad = dot(normed_ref[...], whole, 0, 0).astype(bf16)
    part = grad.shape[1]
    for i in range(blocks_ref.shape[0]):
        blocks_ref[i, :, :part] = grad[16 * i : 16 * i + 8]
        blocks_ref[i, :, part:] = grad[16 * i + 8 : 16 * i + 16]


def grad_blocks(hidden_ref, grad_ref, head_ref, out_ref):
    step = 16
    for first in range(0, PROJ_BLOCKS, step):
        part = dot(hidden_ref[:, 8 * first : 8 * (first + step)], grad_ref[...], 0, 0).astype(bf16)
        for i in range(step):
            near, far = near_far(first + i)
            out_ref[near, 8 * far : 8 * far + 8, :] = part[8 * i : 8 * i + 8]
    for block in range(PROJ_BLOCKS, BLOCKS):
        near, far = near_far(block)
        out_ref[near, 8 * far : 8 * far + 8, :] = head_ref[block - PROJ_BLOCKS]


def chip_sum(kept_ref, other_ref, out_ref):
    out_ref[...] = (kept_ref[...] + other_ref[...].astype(f32)).astype(out_ref.dtype)


def near_sum(pieces_ref, out_ref):
    step = 16
    for first in range(0, out_ref.shape[0], step):
        out_ref[first : first + step] = add_up(pieces_ref.at[:, first : first + step]).astype(out_ref.dtype)


def far_sum(is_proj_ref, pieces_ref, out_ref):
    total = add_up(pieces_ref)
    rows, part = total.shape[0], out_ref.shape[1]

    @pl.when(is_proj_ref[0] == 1)
    def _():
        for row in range(rows):
            out_ref[2 * row : 2 * row + 1, :] = total[row : row + 1, :part]
            out_ref[2 * row + 1 : 2 * row + 2, :] = total[row : row + 1, part:]

    @pl.when(is_proj_ref[0] == 0)
    def _():
        out_ref[:rows, :] = total[:, :part]
        out_ref[rows:, :] = total[:, part:]


def in_vmem(kernel, outs, n_in, scalars=0):
    vmem = pl.BlockSpec(memory_space=pltpu.VMEM)
    smem = pl.BlockSpec(memory_space=pltpu.SMEM)
    return pl.pallas_call(
        kernel,
        out_shape=outs,
        in_specs=[smem] * scalars + [vmem] * n_in,
        out_specs=jax.tree.map(lambda _: vmem, outs),
        compiler_params=pltpu.CompilerParams(vmem_limit_bytes=VMEM_BYTES),
    )


def shape(dims, dtype):
    return jax.ShapeDtypeStruct(dims, dtype)


def local(hidden, in_proj, norm_gain, head_weight, code_ids, stream_mask):
    frames, width = hidden.shape[0], in_proj.shape[1]
    vocab_part = head_weight.shape[1]
    half = frames // 2
    tp = lax.axis_index(TP)
    gain = norm_gain[None, :]
    mine = lax.axis_index("core").reshape(1)
    other = 1 - mine
    code = (code_ids - tp * vocab_part).astype(f32)[None, :]
    mask = stream_mask.astype(f32)[None, :]

    steps, inner = 4, hidden.shape[1]
    sent = pl.pallas_call(
        streamed_product,
        out_shape=shape((half, width), bf16),
        in_specs=[pl.BlockSpec(memory_space=pltpu.SMEM)] + [pl.BlockSpec(memory_space=pltpu.HBM)] * 2,
        out_specs=pl.BlockSpec(memory_space=pltpu.VMEM),
        scratch_shapes=[
            pltpu.VMEM((half, inner), bf16),
            pltpu.VMEM((steps, inner // steps, width), bf16),
            pltpu.SemaphoreType.DMA((steps + 1,)),
        ],
        compiler_params=pltpu.CompilerParams(vmem_limit_bytes=VMEM_BYTES),
    )(other, *(pltpu.with_memory_space_constraint(array, pltpu.HBM) for array in (hidden, in_proj)))
    chip = in_vmem(rows_product_sum, shape((half, width), bf16), 3, 1)(
        mine, hidden, in_proj, lax.ppermute(sent, "core", SWAP)
    )
    x = add_up(lax.all_gather(chip, "xl"))
    inv_rms = lax.rsqrt(jnp.mean(x * x, axis=1, keepdims=True) + norm_eps)
    unit_rows = x * inv_rms
    normed = lax.all_gather((unit_rows * gain).astype(bf16), "core", tiled=True)

    exp_logits, sums = in_vmem(
        exp_rows, [shape((frames, vocab_part), f32), shape((1, frames), f32)], 2
    )(normed, head_weight)
    totals = lax.all_gather(sums, TP, tiled=True)

    rest = (exp_logits, totals, code, mask, head_weight)
    sent = in_vmem(sent_grad, shape((half, width), bf16), 5, 1)(other, *rest)
    kept, head_blocks = in_vmem(
        kept_grad,
        [shape((half, width), f32), shape((BLOCKS - PROJ_BLOCKS, 8, width), bf16)],
        6,
        1,
    )(mine, *rest, normed)
    chip = in_vmem(chip_sum, shape((half, width), bf16), 2)(kept, lax.ppermute(sent, "core", SWAP))
    scaled_grad = add_up(lax.all_gather(chip, "xl")) * gain
    centred = scaled_grad - unit_rows * jnp.mean(scaled_grad * unit_rows, axis=1, keepdims=True)
    row_grad = lax.all_gather((inv_rms * centred).astype(bf16), "core", tiled=True)

    blocks = in_vmem(grad_blocks, shape((N_NEAR, N_FAR * 8, width), bf16), 3)(hidden, row_grad, head_blocks)
    pieces = lax.all_to_all(blocks, NEAR, 0, 0)
    near = in_vmem(near_sum, shape((N_FAR * 8, width), bf16), 1)(pieces)
    far = lax.all_to_all(near.reshape(N_FAR, 8, width), FAR, 0, 0)
    is_proj = (lax.axis_index(SEQ) < PROJ_BLOCKS).astype(jnp.int32).reshape(1)
    weight_grads = in_vmem(far_sum, shape((16, vocab_part), f32), 1, 1)(is_proj, far)

    hidden_grad = pl.pallas_call(
        hidden_rows,
        out_shape=shape((frames, inner), bf16),
        in_specs=[pl.BlockSpec(memory_space=pltpu.VMEM), pl.BlockSpec(memory_space=pltpu.HBM)],
        out_specs=pl.BlockSpec(memory_space=pltpu.VMEM),
        scratch_shapes=[
            pltpu.VMEM((steps, inner // steps, width), bf16),
            pltpu.SemaphoreType.DMA((steps,)),
        ],
        compiler_params=pltpu.CompilerParams(vmem_limit_bytes=VMEM_BYTES),
        cost_estimate=pl.CostEstimate(
            flops=2 * frames * inner * width, transcendentals=0, bytes_accessed=2 * width * (inner + 2 * frames)
        ),
    )(row_grad, pltpu.with_memory_space_constraint(in_proj, pltpu.HBM))
    return (hidden_grad, weight_grads[None])


def solution(mesh):
    fine = Mesh(mesh.devices.reshape(SIZES), AXES)
    in_specs = (P(SEQ, TP), P(TP, None), P(), P(None, TP), P(SEQ), P(SEQ))
    out_specs = (P(SEQ, TP), P(TP, SEQ, None))
    return jax.shard_map(local, mesh=fine, in_specs=in_specs, out_specs=out_specs, check_vma=False)
```

```python
import jax
import jax.numpy as jnp
from jax import lax
from jax.experimental import pallas as pl
from jax.experimental.pallas import tpu as pltpu
from jax.sharding import Mesh
from jax.sharding import PartitionSpec as P

norm_eps = 1e-05
loss_scale = 16.0

AXES = ("yh", "yl", "xh", "zh", "zl", "xl", "core")
SIZES = (4, 2, 2, 6, 2, 2, 2)
SEQ = ("yh", "yl", "xh", "zh", "zl")
TP = ("xl", "core")
NEAR = ("xh", "yl", "zl")
FAR = ("zh", "yh")
N_NEAR = 8
N_FAR = 24
BLOCKS = 192
PROJ_BLOCKS = 128
VMEM_BYTES = 20 << 20
SWAP = [(0, 1), (1, 0)]
f32 = jnp.float32
bf16 = jnp.bfloat16


def dot(a, b, ca, cb):
    return lax.dot_general(a, b, (((ca,), (cb,)), ((), ())), preferred_element_type=f32)


def add_up(pieces):
    total = pieces[0].astype(f32)
    for i in range(1, pieces.shape[0]):
        total = total + pieces[i].astype(f32)
    return total


def near_far(block):
    y, x, z = block // 24, block // 12 % 2, block % 12
    return (x * 2 + y % 2) * 2 + z % 2, z // 2 * 4 + y // 2


def streamed_product(half_ref, a_hbm, b_hbm, sent_ref, kept_ref, a_ref, b_ref, sems):
    rows, steps, depth = sent_ref.shape[0], b_ref.shape[0], b_ref.shape[1]
    copies = [pltpu.make_async_copy(a_hbm, a_ref, sems.at[steps])]
    for i in range(steps):
        copies.append(pltpu.make_async_copy(b_hbm.at[i * depth : (i + 1) * depth, :], b_ref.at[i], sems.at[i]))
    for copy in copies:
        copy.start()
    copies[0].wait()
    mine = pl.ds(pl.multiple_of(half_ref[0] * rows, rows), rows)
    other = pl.ds(pl.multiple_of((1 - half_ref[0]) * rows, rows), rows)
    sent = kept = None
    for i in range(steps):
        copies[1 + i].wait()
        columns = slice(i * depth, (i + 1) * depth)
        sent_part = dot(a_ref[other, columns], b_ref[i], 1, 0)
        kept_part = dot(a_ref[mine, columns], b_ref[i], 1, 0)
        sent = sent_part if i == 0 else sent + sent_part
        kept = kept_part if i == 0 else kept + kept_part
    sent_ref[...] = sent.astype(sent_ref.dtype)
    kept_ref[...] = kept


def hidden_rows(grad_ref, b_hbm, out_ref, b_ref, sems):
    steps, depth = b_ref.shape[0], b_ref.shape[1]
    copies = [
        pltpu.make_async_copy(b_hbm.at[i * depth : (i + 1) * depth, :], b_ref.at[i], sems.at[i]) for i in range(steps)
    ]
    for copy in copies:
        copy.start()
    for i in range(steps):
        copies[i].wait()
        part = loss_scale * dot(grad_ref[...], b_ref[i], 1, 1)
        out_ref[:, i * depth : (i + 1) * depth] = part.astype(out_ref.dtype)


def exp_rows(normed_ref, head_ref, exp_ref, sum_ref):
    exp_logits = jnp.exp(dot(normed_ref[...], head_ref[...], 1, 0))
    exp_ref[...] = exp_logits
    groups = exp_logits[:, :128]
    for start in range(128, exp_logits.shape[1], 128):
        groups = groups + exp_logits[:, start : start + 128]
    sums = lax.dot_general(
        jnp.ones((8, 128), f32), groups, (((1,), (1,)), ((), ())), precision=lax.Precision.HIGHEST, preferred_element_type=f32
    )
    sum_ref[...] = sums[:1]


def spread(rows):
    ones = jnp.ones((rows.shape[0], 128), f32)
    return lax.dot_general(
        rows, ones, (((0,), (0,)), ((), ())), precision=lax.Precision.HIGHEST, preferred_element_type=f32
    )


def dlogit_rows(first, exp_ref, totals_ref, code_ref, mask_ref, rows):
    window = pl.ds(first, rows)
    total, code, weight = (spread(ref[:, window]) for ref in (totals_ref, code_ref, mask_ref))
    scale = weight / total
    parts = []
    for start in range(0, exp_ref.shape[1], 128):
        columns = (lax.broadcasted_iota(jnp.int32, (rows, 128), 1) + start).astype(f32)
        onehot = jnp.where(columns == code, weight, 0.0)
        parts.append((scale * exp_ref[window, start : start + 128] - onehot).astype(bf16))
    return jnp.concatenate(parts, axis=1)


def sent_grad(half_ref, exp_ref, totals_ref, code_ref, mask_ref, head_ref, out_ref):
    rows = out_ref.shape[0]
    start = pl.multiple_of(half_ref[0] * rows, rows)
    dlogit = dlogit_rows(start, exp_ref, totals_ref, code_ref, mask_ref, rows)
    out_ref[...] = dot(dlogit, head_ref[...], 1, 1).astype(out_ref.dtype)


def kept_grad(half_ref, exp_ref, totals_ref, code_ref, mask_ref, head_ref, normed_ref, out_ref, blocks_ref):
    rows = out_ref.shape[0]
    start = pl.multiple_of(half_ref[0] * rows, rows)
    dlogit = dlogit_rows(start, exp_ref, totals_ref, code_ref, mask_ref, rows)
    out_ref[...] = dot(dlogit, head_ref[...], 1, 1)
    whole = dlogit_rows(0, exp_ref, totals_ref, code_ref, mask_ref, exp_ref.shape[0])
    grad = dot(normed_ref[...], whole, 0, 0).astype(bf16)
    part = grad.shape[1]
    for i in range(blocks_ref.shape[0]):
        blocks_ref[i, :, :part] = grad[16 * i : 16 * i + 8]
        blocks_ref[i, :, part:] = grad[16 * i + 8 : 16 * i + 16]


def grad_blocks(hidden_ref, grad_ref, head_ref, out_ref):
    step = 16
    for first in range(0, PROJ_BLOCKS, step):
        part = dot(hidden_ref[:, 8 * first : 8 * (first + step)], grad_ref[...], 0, 0).astype(bf16)
        for i in range(step):
            near, far = near_far(first + i)
            out_ref[near, 8 * far : 8 * far + 8, :] = part[8 * i : 8 * i + 8]
    for block in range(PROJ_BLOCKS, BLOCKS):
        near, far = near_far(block)
        out_ref[near, 8 * far : 8 * far + 8, :] = head_ref[block - PROJ_BLOCKS]


def chip_sum(kept_ref, other_ref, out_ref):
    out_ref[...] = (kept_ref[...] + other_ref[...].astype(f32)).astype(out_ref.dtype)


def near_sum(pieces_ref, out_ref):
    step = 16
    for first in range(0, out_ref.shape[0], step):
        out_ref[first : first + step] = add_up(pieces_ref.at[:, first : first + step]).astype(out_ref.dtype)


def far_sum(is_proj_ref, pieces_ref, out_ref):
    total = add_up(pieces_ref)
    rows, part = total.shape[0], out_ref.shape[1]

    @pl.when(is_proj_ref[0] == 1)
    def _():
        for row in range(rows):
            out_ref[2 * row : 2 * row + 1, :] = total[row : row + 1, :part]
            out_ref[2 * row + 1 : 2 * row + 2, :] = total[row : row + 1, part:]

    @pl.when(is_proj_ref[0] == 0)
    def _():
        out_ref[:rows, :] = total[:, :part]
        out_ref[rows:, :] = total[:, part:]


def in_vmem(kernel, outs, n_in, scalars=0):
    vmem = pl.BlockSpec(memory_space=pltpu.VMEM)
    smem = pl.BlockSpec(memory_space=pltpu.SMEM)
    return pl.pallas_call(
        kernel,
        out_shape=outs,
        in_specs=[smem] * scalars + [vmem] * n_in,
        out_specs=jax.tree.map(lambda _: vmem, outs),
        compiler_params=pltpu.CompilerParams(vmem_limit_bytes=VMEM_BYTES),
    )


def shape(dims, dtype):
    return jax.ShapeDtypeStruct(dims, dtype)


def local(hidden, in_proj, norm_gain, head_weight, code_ids, stream_mask):
    frames, width = hidden.shape[0], in_proj.shape[1]
    vocab_part = head_weight.shape[1]
    half = frames // 2
    tp = lax.axis_index(TP)
    gain = norm_gain[None, :]
    mine = lax.axis_index("core").reshape(1)
    other = 1 - mine
    code = (code_ids - tp * vocab_part).astype(f32)[None, :]
    mask = stream_mask.astype(f32)[None, :]

    steps, inner = 4, hidden.shape[1]
    sent, kept = pl.pallas_call(
        streamed_product,
        out_shape=[shape((half, width), bf16), shape((half, width), f32)],
        in_specs=[pl.BlockSpec(memory_space=pltpu.SMEM)] + [pl.BlockSpec(memory_space=pltpu.HBM)] * 2,
        out_specs=[pl.BlockSpec(memory_space=pltpu.VMEM)] * 2,
        scratch_shapes=[
            pltpu.VMEM((frames, inner), bf16),
            pltpu.VMEM((steps, inner // steps, width), bf16),
            pltpu.SemaphoreType.DMA((steps + 1,)),
        ],
        compiler_params=pltpu.CompilerParams(vmem_limit_bytes=VMEM_BYTES),
    )(mine, *(pltpu.with_memory_space_constraint(array, pltpu.HBM) for array in (hidden, in_proj)))
    chip = in_vmem(chip_sum, shape((half, width), bf16), 2)(kept, lax.ppermute(sent, "core", SWAP))
    x = add_up(lax.all_gather(chip, "xl"))
    inv_rms = lax.rsqrt(jnp.mean(x * x, axis=1, keepdims=True) + norm_eps)
    unit_rows = x * inv_rms
    normed = lax.all_gather((unit_rows * gain).astype(bf16), "core", tiled=True)

    exp_logits, sums = in_vmem(
        exp_rows, [shape((frames, vocab_part), f32), shape((1, frames), f32)], 2
    )(normed, head_weight)
    totals = lax.all_gather(sums, TP, tiled=True)

    rest = (exp_logits, totals, code, mask, head_weight)
    sent = in_vmem(sent_grad, shape((half, width), bf16), 5, 1)(other, *rest)
    kept, head_blocks = in_vmem(
        kept_grad,
        [shape((half, width), f32), shape((BLOCKS - PROJ_BLOCKS, 8, width), bf16)],
        6,
        1,
    )(mine, *rest, normed)
    chip = in_vmem(chip_sum, shape((half, width), bf16), 2)(kept, lax.ppermute(sent, "core", SWAP))
    scaled_grad = add_up(lax.all_gather(chip, "xl")) * gain
    centred = scaled_grad - unit_rows * jnp.mean(scaled_grad * unit_rows, axis=1, keepdims=True)
    row_grad = lax.all_gather((inv_rms * centred).astype(bf16), "core", tiled=True)

    blocks = in_vmem(grad_blocks, shape((N_NEAR, N_FAR * 8, width), bf16), 3)(hidden, row_grad, head_blocks)
    pieces = lax.all_to_all(blocks, NEAR, 0, 0)
    near = in_vmem(near_sum, shape((N_FAR * 8, width), bf16), 1)(pieces)
    far = lax.all_to_all(near.reshape(N_FAR, 8, width), FAR, 0, 0)
    is_proj = (lax.axis_index(SEQ) < PROJ_BLOCKS).astype(jnp.int32).reshape(1)
    weight_grads = in_vmem(far_sum, shape((16, vocab_part), f32), 1, 1)(is_proj, far)

    hidden_grad = pl.pallas_call(
        hidden_rows,
        out_shape=shape((frames, inner), bf16),
        in_specs=[pl.BlockSpec(memory_space=pltpu.VMEM), pl.BlockSpec(memory_space=pltpu.HBM)],
        out_specs=pl.BlockSpec(memory_space=pltpu.VMEM),
        scratch_shapes=[
            pltpu.VMEM((steps, inner // steps, width), bf16),
            pltpu.SemaphoreType.DMA((steps,)),
        ],
        compiler_params=pltpu.CompilerParams(vmem_limit_bytes=VMEM_BYTES),
        cost_estimate=pl.CostEstimate(
            flops=2 * frames * inner * width, transcendentals=0, bytes_accessed=2 * width * (inner + 2 * frames)
        ),
    )(row_grad, pltpu.with_memory_space_constraint(in_proj, pltpu.HBM))
    return (hidden_grad, weight_grads[None])


def solution(mesh):
    fine = Mesh(mesh.devices.reshape(SIZES), AXES)
    in_specs = (P(SEQ, TP), P(TP, None), P(), P(None, TP), P(SEQ), P(SEQ))
    out_specs = (P(SEQ, TP), P(TP, SEQ, None))
    return jax.shard_map(local, mesh=fine, in_specs=in_specs, out_specs=out_specs, check_vma=False)
```

```python
import jax
import jax.numpy as jnp
from jax import lax
from jax.experimental import pallas as pl
from jax.experimental.pallas import tpu as pltpu
from jax.sharding import Mesh
from jax.sharding import PartitionSpec as P

norm_eps = 1e-05
loss_scale = 16.0

AXES = ("yh", "yl", "xh", "zh", "zl", "xl", "core")
SIZES = (4, 2, 2, 6, 2, 2, 2)
SEQ = ("yh", "yl", "xh", "zh", "zl")
TP = ("xl", "core")
NEAR = ("xh", "yl", "zl")
FAR = ("zh", "yh")
N_NEAR = 8
N_FAR = 24
BLOCKS = 192
PROJ_BLOCKS = 128
LATE_BLOCKS = 144
EARLY = ("yl", "zl")
VMEM_BYTES = 20 << 20
SWAP = [(0, 1), (1, 0)]
f32 = jnp.float32
bf16 = jnp.bfloat16


def dot(a, b, ca, cb):
    return lax.dot_general(a, b, (((ca,), (cb,)), ((), ())), preferred_element_type=f32)


def add_up(pieces):
    total = pieces[0].astype(f32)
    for i in range(1, pieces.shape[0]):
        total = total + pieces[i].astype(f32)
    return total


def place(block):
    y, x, z = block // 24, block // 12 % 2, block % 12
    return y // 2, y % 2, x, z // 2, z % 2


def streamed_product(half_ref, a_hbm, b_hbm, sent_ref, kept_ref, a_ref, b_ref, sems):
    rows, steps, depth = sent_ref.shape[0], b_ref.shape[0], b_ref.shape[1]
    copies = [pltpu.make_async_copy(a_hbm, a_ref, sems.at[steps])]
    for i in range(steps):
        copies.append(pltpu.make_async_copy(b_hbm.at[i * depth : (i + 1) * depth, :], b_ref.at[i], sems.at[i]))
    for copy in copies:
        copy.start()
    copies[0].wait()
    mine = pl.ds(pl.multiple_of(half_ref[0] * rows, rows), rows)
    other = pl.ds(pl.multiple_of((1 - half_ref[0]) * rows, rows), rows)
    sent = kept = None
    for i in range(steps):
        copies[1 + i].wait()
        columns = slice(i * depth, (i + 1) * depth)
        sent_part = dot(a_ref[other, columns], b_ref[i], 1, 0)
        kept_part = dot(a_ref[mine, columns], b_ref[i], 1, 0)
        sent = sent_part if i == 0 else sent + sent_part
        kept = kept_part if i == 0 else kept + kept_part
    sent_ref[...] = sent.astype(sent_ref.dtype)
    kept_ref[...] = kept


def hidden_rows(grad_ref, b_hbm, out_ref, b_ref, sems):
    steps, depth = b_ref.shape[0], b_ref.shape[1]
    copies = [
        pltpu.make_async_copy(b_hbm.at[i * depth : (i + 1) * depth, :], b_ref.at[i], sems.at[i]) for i in range(steps)
    ]
    for copy in copies:
        copy.start()
    for i in range(steps):
        copies[i].wait()
        part = loss_scale * dot(grad_ref[...], b_ref[i], 1, 1)
        out_ref[:, i * depth : (i + 1) * depth] = part.astype(out_ref.dtype)


def exp_rows(normed_ref, head_ref, exp_ref, sum_ref):
    exp_logits = jnp.exp(dot(normed_ref[...], head_ref[...], 1, 0))
    exp_ref[...] = exp_logits
    groups = exp_logits[:, :128]
    for start in range(128, exp_logits.shape[1], 128):
        groups = groups + exp_logits[:, start : start + 128]
    sums = lax.dot_general(
        jnp.ones((8, 128), f32), groups, (((1,), (1,)), ((), ())), precision=lax.Precision.HIGHEST, preferred_element_type=f32
    )
    sum_ref[...] = sums[:1]


def spread(rows):
    ones = jnp.ones((rows.shape[0], 128), f32)
    return lax.dot_general(
        rows, ones, (((0,), (0,)), ((), ())), precision=lax.Precision.HIGHEST, preferred_element_type=f32
    )


def dlogit_rows(first, exp_ref, totals_ref, code_ref, mask_ref, rows):
    window = pl.ds(first, rows)
    total, code, weight = (spread(ref[:, window]) for ref in (totals_ref, code_ref, mask_ref))
    scale = weight / total
    parts = []
    for start in range(0, exp_ref.shape[1], 128):
        columns = (lax.broadcasted_iota(jnp.int32, (rows, 128), 1) + start).astype(f32)
        onehot = jnp.where(columns == code, weight, 0.0)
        parts.append((scale * exp_ref[window, start : start + 128] - onehot).astype(bf16))
    return jnp.concatenate(parts, axis=1)


def sent_grad(half_ref, exp_ref, totals_ref, code_ref, mask_ref, head_ref, out_ref):
    rows = out_ref.shape[0]
    start = pl.multiple_of(half_ref[0] * rows, rows)
    dlogit = dlogit_rows(start, exp_ref, totals_ref, code_ref, mask_ref, rows)
    out_ref[...] = dot(dlogit, head_ref[...], 1, 1).astype(out_ref.dtype)


def kept_grad(half_ref, exp_ref, totals_ref, code_ref, mask_ref, head_ref, normed_ref, out_ref, late_ref, early_ref):
    rows = out_ref.shape[0]
    start = pl.multiple_of(half_ref[0] * rows, rows)
    dlogit = dlogit_rows(start, exp_ref, totals_ref, code_ref, mask_ref, rows)
    out_ref[...] = dot(dlogit, head_ref[...], 1, 1)
    whole = dlogit_rows(0, exp_ref, totals_ref, code_ref, mask_ref, exp_ref.shape[0])
    grad = dot(normed_ref[...], whole, 0, 0).astype(bf16)
    part = grad.shape[1]
    for i in range(BLOCKS - PROJ_BLOCKS):
        top, bottom = grad[16 * i : 16 * i + 8], grad[16 * i + 8 : 16 * i + 16]
        if PROJ_BLOCKS + i < LATE_BLOCKS:
            late_ref[i, :, :part] = top
            late_ref[i, :, part:] = bottom
        else:
            _, yl, xh, zh, zl = place(PROJ_BLOCKS + i)
            row = 8 * (xh * 6 + zh)
            early_ref[2 * yl + zl, row : row + 8, :part] = top
            early_ref[2 * yl + zl, row : row + 8, part:] = bottom


def grad_blocks(hidden_ref, grad_ref, head_ref, out_ref):
    step = 16
    for first in range(0, LATE_BLOCKS, step):
        if first < PROJ_BLOCKS:
            part = dot(hidden_ref[:, 8 * first : 8 * (first + step)], grad_ref[...], 0, 0).astype(bf16)
        for i in range(step):
            yh, yl, xh, zh, zl = place(first + i)
            row = 8 * (zh * 3 + yh)
            block = part[8 * i : 8 * i + 8] if first < PROJ_BLOCKS else head_ref[i]
            out_ref[(xh * 2 + yl) * 2 + zl, row : row + 8, :] = block


def early_sum(half_ref, pieces_ref, sent_ref, kept_ref):
    rows = sent_ref.shape[0]
    mine = pl.ds(pl.multiple_of(half_ref[0] * rows, rows), rows)
    other = pl.ds(pl.multiple_of((1 - half_ref[0]) * rows, rows), rows)
    sent_ref[...] = add_up(pieces_ref.at[:, other]).astype(sent_ref.dtype)
    kept_ref[...] = add_up(pieces_ref.at[:, mine])


def chip_sum(kept_ref, other_ref, out_ref):
    out_ref[...] = (kept_ref[...] + other_ref[...].astype(f32)).astype(out_ref.dtype)


def near_sum(pieces_ref, kept_ref, other_ref, out_ref):
    for zh in range(6):
        window = slice(24 * zh, 24 * zh + 24)
        out_ref[32 * zh : 32 * zh + 24] = add_up(pieces_ref.at[:, window]).astype(out_ref.dtype)
        window = slice(8 * zh, 8 * zh + 8)
        early = kept_ref[window] + other_ref[window].astype(f32)
        out_ref[32 * zh + 24 : 32 * zh + 32] = early.astype(out_ref.dtype)


def far_sum(is_proj_ref, pieces_ref, out_ref):
    total = add_up(pieces_ref)
    rows, part = total.shape[0], out_ref.shape[1]

    @pl.when(is_proj_ref[0] == 1)
    def _():
        for row in range(rows):
            out_ref[2 * row : 2 * row + 1, :] = total[row : row + 1, :part]
            out_ref[2 * row + 1 : 2 * row + 2, :] = total[row : row + 1, part:]

    @pl.when(is_proj_ref[0] == 0)
    def _():
        out_ref[:rows, :] = total[:, :part]
        out_ref[rows:, :] = total[:, part:]


def in_vmem(kernel, outs, n_in, scalars=0):
    vmem = pl.BlockSpec(memory_space=pltpu.VMEM)
    smem = pl.BlockSpec(memory_space=pltpu.SMEM)
    return pl.pallas_call(
        kernel,
        out_shape=outs,
        in_specs=[smem] * scalars + [vmem] * n_in,
        out_specs=jax.tree.map(lambda _: vmem, outs),
        compiler_params=pltpu.CompilerParams(vmem_limit_bytes=VMEM_BYTES),
    )


def shape(dims, dtype):
    return jax.ShapeDtypeStruct(dims, dtype)


def local(hidden, in_proj, norm_gain, head_weight, code_ids, stream_mask):
    frames, width = hidden.shape[0], in_proj.shape[1]
    vocab_part = head_weight.shape[1]
    half = frames // 2
    tp = lax.axis_index(TP)
    gain = norm_gain[None, :]
    mine = lax.axis_index("core").reshape(1)
    other = 1 - mine
    code = (code_ids - tp * vocab_part).astype(f32)[None, :]
    mask = stream_mask.astype(f32)[None, :]

    steps, inner = 4, hidden.shape[1]
    sent, kept = pl.pallas_call(
        streamed_product,
        out_shape=[shape((half, width), bf16), shape((half, width), f32)],
        in_specs=[pl.BlockSpec(memory_space=pltpu.SMEM)] + [pl.BlockSpec(memory_space=pltpu.HBM)] * 2,
        out_specs=[pl.BlockSpec(memory_space=pltpu.VMEM)] * 2,
        scratch_shapes=[
            pltpu.VMEM((frames, inner), bf16),
            pltpu.VMEM((steps, inner // steps, width), bf16),
            pltpu.SemaphoreType.DMA((steps + 1,)),
        ],
        compiler_params=pltpu.CompilerParams(vmem_limit_bytes=VMEM_BYTES),
    )(mine, *(pltpu.with_memory_space_constraint(array, pltpu.HBM) for array in (hidden, in_proj)))
    chip = in_vmem(chip_sum, shape((half, width), bf16), 2)(kept, lax.ppermute(sent, "core", SWAP))
    x = add_up(lax.all_gather(chip, "xl"))
    inv_rms = lax.rsqrt(jnp.mean(x * x, axis=1, keepdims=True) + norm_eps)
    unit_rows = x * inv_rms
    normed = lax.all_gather((unit_rows * gain).astype(bf16), "core", tiled=True)

    exp_logits, sums = in_vmem(
        exp_rows, [shape((frames, vocab_part), f32), shape((1, frames), f32)], 2
    )(normed, head_weight)
    totals = lax.all_gather(sums, TP, tiled=True)

    rest = (exp_logits, totals, code, mask, head_weight)
    sent = in_vmem(sent_grad, shape((half, width), bf16), 5, 1)(other, *rest)
    exp_logits, sent = lax.optimization_barrier((exp_logits, sent))
    rest = (exp_logits, *rest[1:])
    kept, late_head, early = in_vmem(
        kept_grad,
        [
            shape((half, width), f32),
            shape((LATE_BLOCKS - PROJ_BLOCKS, 8, width), bf16),
            shape((4, 96, width), bf16),
        ],
        6,
        1,
    )(mine, *rest, normed)
    early = lax.all_to_all(early, EARLY, 0, 0)
    chip = in_vmem(chip_sum, shape((half, width), bf16), 2)(kept, lax.ppermute(sent, "core", SWAP))
    scaled_grad = add_up(lax.all_gather(chip, "xl")) * gain
    centred = scaled_grad - unit_rows * jnp.mean(scaled_grad * unit_rows, axis=1, keepdims=True)
    row_grad = lax.all_gather((inv_rms * centred).astype(bf16), "core", tiled=True)

    blocks = in_vmem(grad_blocks, shape((N_NEAR, LATE_BLOCKS, width), bf16), 3)(hidden, row_grad, late_head)
    early_out = [shape((48, width), bf16), shape((48, width), f32)]
    early_sent, early_kept = in_vmem(early_sum, early_out, 1, 1)(lax.axis_index("xh").reshape(1), early)
    blocks, early_sent = lax.optimization_barrier((blocks, early_sent))
    pieces = lax.all_to_all(blocks, NEAR, 0, 0)
    early_other = lax.ppermute(early_sent, "xh", SWAP)
    near = in_vmem(near_sum, shape((N_FAR * 8, width), bf16), 3)(
        pieces, early_kept, early_other
    )
    far = lax.all_to_all(near.reshape(N_FAR, 8, width), FAR, 0, 0)
    is_proj = (lax.axis_index(SEQ) < PROJ_BLOCKS).astype(jnp.int32).reshape(1)
    weight_grads = in_vmem(far_sum, shape((16, vocab_part), f32), 1, 1)(is_proj, far)

    hidden_grad = pl.pallas_call(
        hidden_rows,
        out_shape=shape((frames, inner), bf16),
        in_specs=[pl.BlockSpec(memory_space=pltpu.VMEM), pl.BlockSpec(memory_space=pltpu.HBM)],
        out_specs=pl.BlockSpec(memory_space=pltpu.VMEM),
        scratch_shapes=[
            pltpu.VMEM((steps, inner // steps, width), bf16),
            pltpu.SemaphoreType.DMA((steps,)),
        ],
        compiler_params=pltpu.CompilerParams(vmem_limit_bytes=VMEM_BYTES),
        cost_estimate=pl.CostEstimate(
            flops=2 * frames * inner * width, transcendentals=0, bytes_accessed=2 * width * (inner + 2 * frames)
        ),
    )(row_grad, pltpu.with_memory_space_constraint(in_proj, pltpu.HBM))
    return (hidden_grad, weight_grads[None])


def solution(mesh):
    fine = Mesh(mesh.devices.reshape(SIZES), AXES)
    in_specs = (P(SEQ, TP), P(TP, None), P(), P(None, TP), P(SEQ), P(SEQ))
    out_specs = (P(SEQ, TP), P(TP, SEQ, None))
    return jax.shard_map(local, mesh=fine, in_specs=in_specs, out_specs=out_specs, check_vma=False)
```

```python
import jax
import jax.numpy as jnp
from jax import lax
from jax.experimental import pallas as pl
from jax.experimental.pallas import tpu as pltpu
from jax.sharding import Mesh
from jax.sharding import PartitionSpec as P

norm_eps = 1e-05
loss_scale = 16.0

AXES = ("yh", "yl", "xh", "zh", "zl", "xl", "core")
SIZES = (4, 2, 2, 6, 2, 2, 2)
SEQ = ("yh", "yl", "xh", "zh", "zl")
TP = ("xl", "core")
NEAR = ("xh", "yl", "zl")
FAR = ("zh", "yh")
N_NEAR = 8
N_FAR = 24
BLOCKS = 192
PROJ_BLOCKS = 128
LATE_BLOCKS = 144
EARLY = ("yl", "zl")
VMEM_BYTES = 20 << 20
SWAP = [(0, 1), (1, 0)]
f32 = jnp.float32
bf16 = jnp.bfloat16


def dot(a, b, ca, cb):
    return lax.dot_general(a, b, (((ca,), (cb,)), ((), ())), preferred_element_type=f32)


def add_up(pieces):
    total = pieces[0].astype(f32)
    for i in range(1, pieces.shape[0]):
        total = total + pieces[i].astype(f32)
    return total


def place(block):
    y, x, z = block // 24, block // 12 % 2, block % 12
    return y // 2, y % 2, x, z // 2, z % 2


def streamed_product(half_ref, a_hbm, b_hbm, sent_ref, kept_ref, a_ref, b_ref, sems):
    rows, steps, depth = sent_ref.shape[0], b_ref.shape[0], b_ref.shape[1]
    copies = [pltpu.make_async_copy(a_hbm, a_ref, sems.at[steps])]
    for i in range(steps):
        copies.append(pltpu.make_async_copy(b_hbm.at[i * depth : (i + 1) * depth, :], b_ref.at[i], sems.at[i]))
    for copy in copies:
        copy.start()
    copies[0].wait()
    mine = pl.ds(pl.multiple_of(half_ref[0] * rows, rows), rows)
    other = pl.ds(pl.multiple_of((1 - half_ref[0]) * rows, rows), rows)
    sent = kept = None
    for i in range(steps):
        copies[1 + i].wait()
        columns = slice(i * depth, (i + 1) * depth)
        sent_part = dot(a_ref[other, columns], b_ref[i], 1, 0)
        kept_part = dot(a_ref[mine, columns], b_ref[i], 1, 0)
        sent = sent_part if i == 0 else sent + sent_part
        kept = kept_part if i == 0 else kept + kept_part
    sent_ref[...] = sent.astype(sent_ref.dtype)
    kept_ref[...] = kept


def hidden_rows(grad_ref, b_hbm, out_ref, b_ref, sems):
    steps, depth = b_ref.shape[0], b_ref.shape[1]
    copies = [
        pltpu.make_async_copy(b_hbm.at[i * depth : (i + 1) * depth, :], b_ref.at[i], sems.at[i]) for i in range(steps)
    ]
    for copy in copies:
        copy.start()
    for i in range(steps):
        copies[i].wait()
        part = loss_scale * dot(grad_ref[...], b_ref[i], 1, 1)
        out_ref[:, i * depth : (i + 1) * depth] = part.astype(out_ref.dtype)


def exp_rows(normed_ref, head_ref, exp_ref, sum_ref):
    exp_logits = jnp.exp(dot(normed_ref[...], head_ref[...], 1, 0))
    exp_ref[...] = exp_logits
    groups = exp_logits[:, :128]
    for start in range(128, exp_logits.shape[1], 128):
        groups = groups + exp_logits[:, start : start + 128]
    sums = lax.dot_general(
        jnp.ones((8, 128), f32), groups, (((1,), (1,)), ((), ())), precision=lax.Precision.HIGHEST, preferred_element_type=f32
    )
    sum_ref[...] = sums[:1]


def spread(rows):
    ones = jnp.ones((rows.shape[0], 128), f32)
    return lax.dot_general(
        rows, ones, (((0,), (0,)), ((), ())), precision=lax.Precision.HIGHEST, preferred_element_type=f32
    )


def dlogit_rows(first, exp_ref, totals_ref, code_ref, mask_ref, rows):
    window = pl.ds(first, rows)
    total, code, weight = (spread(ref[:, window]) for ref in (totals_ref, code_ref, mask_ref))
    scale = weight / total
    parts = []
    for start in range(0, exp_ref.shape[1], 128):
        columns = (lax.broadcasted_iota(jnp.int32, (rows, 128), 1) + start).astype(f32)
        onehot = jnp.where(columns == code, weight, 0.0)
        parts.append((scale * exp_ref[window, start : start + 128] - onehot).astype(bf16))
    return jnp.concatenate(parts, axis=1)


def sent_grad(half_ref, exp_ref, totals_ref, code_ref, mask_ref, head_ref, out_ref):
    rows = out_ref.shape[0]
    start = pl.multiple_of(half_ref[0] * rows, rows)
    dlogit = dlogit_rows(start, exp_ref, totals_ref, code_ref, mask_ref, rows)
    out_ref[...] = dot(dlogit, head_ref[...], 1, 1).astype(out_ref.dtype)


def kept_grad(half_ref, exp_ref, totals_ref, code_ref, mask_ref, head_ref, normed_ref, out_ref, late_ref, early_ref):
    rows = out_ref.shape[0]
    start = pl.multiple_of(half_ref[0] * rows, rows)
    dlogit = dlogit_rows(start, exp_ref, totals_ref, code_ref, mask_ref, rows)
    out_ref[...] = dot(dlogit, head_ref[...], 1, 1)
    whole = dlogit_rows(0, exp_ref, totals_ref, code_ref, mask_ref, exp_ref.shape[0])
    grad = dot(normed_ref[...], whole, 0, 0).astype(bf16)
    part = grad.shape[1]
    for i in range(BLOCKS - PROJ_BLOCKS):
        top, bottom = grad[16 * i : 16 * i + 8], grad[16 * i + 8 : 16 * i + 16]
        if PROJ_BLOCKS + i < LATE_BLOCKS:
            late_ref[i, :, :part] = top
            late_ref[i, :, part:] = bottom
        else:
            _, yl, xh, zh, zl = place(PROJ_BLOCKS + i)
            row = 8 * (xh * 6 + zh)
            early_ref[2 * yl + zl, row : row + 8, :part] = top
            early_ref[2 * yl + zl, row : row + 8, part:] = bottom


def grad_blocks(hidden_ref, grad_ref, head_ref, out_ref):
    step = 16
    for first in range(0, LATE_BLOCKS, step):
        if first < PROJ_BLOCKS:
            part = dot(hidden_ref[:, 8 * first : 8 * (first + step)], grad_ref[...], 0, 0).astype(bf16)
        for i in range(step):
            yh, yl, xh, zh, zl = place(first + i)
            row = 8 * (zh * 3 + yh)
            block = part[8 * i : 8 * i + 8] if first < PROJ_BLOCKS else head_ref[i]
            out_ref[(xh * 2 + yl) * 2 + zl, row : row + 8, :] = block


def early_sum(half_ref, pieces_ref, sent_ref, kept_ref):
    rows = sent_ref.shape[0]
    mine = pl.ds(pl.multiple_of(half_ref[0] * rows, rows), rows)
    other = pl.ds(pl.multiple_of((1 - half_ref[0]) * rows, rows), rows)
    sent_ref[...] = add_up(pieces_ref.at[:, other]).astype(sent_ref.dtype)
    kept_ref[...] = add_up(pieces_ref.at[:, mine])


def chip_sum(kept_ref, other_ref, out_ref):
    out_ref[...] = (kept_ref[...] + other_ref[...].astype(f32)).astype(out_ref.dtype)


def near_sum(pieces_ref, kept_ref, other_ref, out_ref):
    for zh in range(6):
        window = slice(24 * zh, 24 * zh + 24)
        out_ref[32 * zh : 32 * zh + 24] = add_up(pieces_ref.at[:, window]).astype(out_ref.dtype)
        window = slice(8 * zh, 8 * zh + 8)
        early = kept_ref[window] + other_ref[window].astype(f32)
        out_ref[32 * zh + 24 : 32 * zh + 32] = early.astype(out_ref.dtype)


def far_sum(is_proj_ref, pieces_ref, out_ref):
    total = add_up(pieces_ref)
    rows, part = total.shape[0], out_ref.shape[1]

    @pl.when(is_proj_ref[0] == 1)
    def _():
        for row in range(rows):
            out_ref[2 * row : 2 * row + 1, :] = total[row : row + 1, :part]
            out_ref[2 * row + 1 : 2 * row + 2, :] = total[row : row + 1, part:]

    @pl.when(is_proj_ref[0] == 0)
    def _():
        out_ref[:rows, :] = total[:, :part]
        out_ref[rows:, :] = total[:, part:]


def in_vmem(kernel, outs, n_in, scalars=0):
    vmem = pl.BlockSpec(memory_space=pltpu.VMEM)
    smem = pl.BlockSpec(memory_space=pltpu.SMEM)
    return pl.pallas_call(
        kernel,
        out_shape=outs,
        in_specs=[smem] * scalars + [vmem] * n_in,
        out_specs=jax.tree.map(lambda _: vmem, outs),
        compiler_params=pltpu.CompilerParams(vmem_limit_bytes=VMEM_BYTES),
    )


def shape(dims, dtype):
    return jax.ShapeDtypeStruct(dims, dtype)


def local(hidden, in_proj, norm_gain, head_weight, code_ids, stream_mask):
    frames, width = hidden.shape[0], in_proj.shape[1]
    vocab_part = head_weight.shape[1]
    half = frames // 2
    tp = lax.axis_index(TP)
    gain = norm_gain[None, :]
    mine = lax.axis_index("core").reshape(1)
    other = 1 - mine
    code = (code_ids - tp * vocab_part).astype(f32)[None, :]
    mask = stream_mask.astype(f32)[None, :]

    steps, inner = 4, hidden.shape[1]
    sent, kept = pl.pallas_call(
        streamed_product,
        out_shape=[shape((half, width), bf16), shape((half, width), f32)],
        in_specs=[pl.BlockSpec(memory_space=pltpu.SMEM)] + [pl.BlockSpec(memory_space=pltpu.HBM)] * 2,
        out_specs=[pl.BlockSpec(memory_space=pltpu.VMEM)] * 2,
        scratch_shapes=[
            pltpu.VMEM((frames, inner), bf16),
            pltpu.VMEM((steps, inner // steps, width), bf16),
            pltpu.SemaphoreType.DMA((steps + 1,)),
        ],
        compiler_params=pltpu.CompilerParams(vmem_limit_bytes=VMEM_BYTES),
    )(mine, *(pltpu.with_memory_space_constraint(array, pltpu.HBM) for array in (hidden, in_proj)))
    chip = in_vmem(chip_sum, shape((half, width), bf16), 2)(kept, lax.ppermute(sent, "core", SWAP))
    x = add_up(lax.all_gather(chip, "xl"))
    inv_rms = lax.rsqrt(jnp.mean(x * x, axis=1, keepdims=True) + norm_eps)
    unit_rows = x * inv_rms
    normed = lax.all_gather((unit_rows * gain).astype(bf16), "core", tiled=True)

    exp_logits, sums = in_vmem(
        exp_rows, [shape((frames, vocab_part), f32), shape((1, frames), f32)], 2
    )(normed, head_weight)
    totals = lax.all_gather(sums, TP, tiled=True)

    rest = (exp_logits, totals, code, mask, head_weight)
    sent = in_vmem(sent_grad, shape((half, width), bf16), 5, 1)(other, *rest)
    exp_logits, sent = lax.optimization_barrier((exp_logits, sent))
    rest = (exp_logits, *rest[1:])
    kept, late_head, early = in_vmem(
        kept_grad,
        [
            shape((half, width), f32),
            shape((LATE_BLOCKS - PROJ_BLOCKS, 8, width), bf16),
            shape((4, 96, width), bf16),
        ],
        6,
        1,
    )(mine, *rest, normed)
    early, swapped = lax.optimization_barrier((early, lax.ppermute(sent, "core", SWAP)))
    early = lax.all_to_all(early, EARLY, 0, 0)
    chip = in_vmem(chip_sum, shape((half, width), bf16), 2)(kept, swapped)
    scaled_grad = add_up(lax.all_gather(chip, "xl")) * gain
    centred = scaled_grad - unit_rows * jnp.mean(scaled_grad * unit_rows, axis=1, keepdims=True)
    row_grad = lax.all_gather((inv_rms * centred).astype(bf16), "core", tiled=True)

    blocks = in_vmem(grad_blocks, shape((N_NEAR, LATE_BLOCKS, width), bf16), 3)(hidden, row_grad, late_head)
    early_out = [shape((48, width), bf16), shape((48, width), f32)]
    early_sent, early_kept = in_vmem(early_sum, early_out, 1, 1)(lax.axis_index("xh").reshape(1), early)
    blocks, early_sent = lax.optimization_barrier((blocks, early_sent))
    pieces = lax.all_to_all(blocks, NEAR, 0, 0)
    early_other = lax.ppermute(early_sent, "xh", SWAP)
    near = in_vmem(near_sum, shape((N_FAR * 8, width), bf16), 3)(
        pieces, early_kept, early_other
    )
    far = lax.all_to_all(near.reshape(N_FAR, 8, width), FAR, 0, 0)
    is_proj = (lax.axis_index(SEQ) < PROJ_BLOCKS).astype(jnp.int32).reshape(1)
    weight_grads = in_vmem(far_sum, shape((16, vocab_part), f32), 1, 1)(is_proj, far)

    hidden_grad = pl.pallas_call(
        hidden_rows,
        out_shape=shape((frames, inner), bf16),
        in_specs=[pl.BlockSpec(memory_space=pltpu.VMEM), pl.BlockSpec(memory_space=pltpu.HBM)],
        out_specs=pl.BlockSpec(memory_space=pltpu.VMEM),
        scratch_shapes=[
            pltpu.VMEM((steps, inner // steps, width), bf16),
            pltpu.SemaphoreType.DMA((steps,)),
        ],
        compiler_params=pltpu.CompilerParams(vmem_limit_bytes=VMEM_BYTES),
        cost_estimate=pl.CostEstimate(
            flops=2 * frames * inner * width, transcendentals=0, bytes_accessed=2 * width * (inner + 2 * frames)
        ),
    )(row_grad, pltpu.with_memory_space_constraint(in_proj, pltpu.HBM))
    return (hidden_grad, weight_grads[None])


def solution(mesh):
    fine = Mesh(mesh.devices.reshape(SIZES), AXES)
    in_specs = (P(SEQ, TP), P(TP, None), P(), P(None, TP), P(SEQ), P(SEQ))
    out_specs = (P(SEQ, TP), P(TP, SEQ, None))
    return jax.shard_map(local, mesh=fine, in_specs=in_specs, out_specs=out_specs, check_vma=False)
```

```python
import jax
import jax.numpy as jnp
from jax import lax
from jax.experimental import pallas as pl
from jax.experimental.pallas import tpu as pltpu
from jax.sharding import Mesh
from jax.sharding import PartitionSpec as P

norm_eps = 1e-05
loss_scale = 16.0

AXES = ("yh", "yl", "xh", "zh", "zl", "xl", "core")
SIZES = (4, 2, 2, 6, 2, 2, 2)
SEQ = ("yh", "yl", "xh", "zh", "zl")
TP = ("xl", "core")
NEAR = ("xh", "yl", "zl")
FAR = ("zh", "yh")
N_NEAR = 8
N_FAR = 24
BLOCKS = 192
PROJ_BLOCKS = 128
LATE_BLOCKS = 144
EARLY = ("yl", "zl")
VMEM_BYTES = 20 << 20
SWAP = [(0, 1), (1, 0)]
f32 = jnp.float32
bf16 = jnp.bfloat16


def dot(a, b, ca, cb):
    return lax.dot_general(a, b, (((ca,), (cb,)), ((), ())), preferred_element_type=f32)


def add_up(pieces):
    total = pieces[0].astype(f32)
    for i in range(1, pieces.shape[0]):
        total = total + pieces[i].astype(f32)
    return total


def place(block):
    y, x, z = block // 24, block // 12 % 2, block % 12
    return y // 2, y % 2, x, z // 2, z % 2


def streamed_product(half_ref, a_hbm, b_hbm, sent_ref, kept_ref, a_ref, b_ref, sems):
    rows, steps, depth = sent_ref.shape[0], b_ref.shape[0], b_ref.shape[1]
    copies = [pltpu.make_async_copy(a_hbm, a_ref, sems.at[steps])]
    for i in range(steps):
        copies.append(pltpu.make_async_copy(b_hbm.at[i * depth : (i + 1) * depth, :], b_ref.at[i], sems.at[i]))
    for copy in copies:
        copy.start()
    copies[0].wait()
    mine = pl.ds(pl.multiple_of(half_ref[0] * rows, rows), rows)
    other = pl.ds(pl.multiple_of((1 - half_ref[0]) * rows, rows), rows)
    sent = kept = None
    for i in range(steps):
        copies[1 + i].wait()
        columns = slice(i * depth, (i + 1) * depth)
        sent_part = dot(a_ref[other, columns], b_ref[i], 1, 0)
        kept_part = dot(a_ref[mine, columns], b_ref[i], 1, 0)
        sent = sent_part if i == 0 else sent + sent_part
        kept = kept_part if i == 0 else kept + kept_part
    sent_ref[...] = sent.astype(sent_ref.dtype)
    kept_ref[...] = kept


def hidden_rows(grad_ref, b_hbm, out_ref, b_ref, sems):
    steps, depth = b_ref.shape[0], b_ref.shape[1]
    copies = [
        pltpu.make_async_copy(b_hbm.at[i * depth : (i + 1) * depth, :], b_ref.at[i], sems.at[i]) for i in range(steps)
    ]
    for copy in copies:
        copy.start()
    for i in range(steps):
        copies[i].wait()
        part = loss_scale * dot(grad_ref[...], b_ref[i], 1, 1)
        out_ref[:, i * depth : (i + 1) * depth] = part.astype(out_ref.dtype)


def exp_rows(normed_ref, head_ref, exp_ref, sum_ref):
    exp_logits = jnp.exp(dot(normed_ref[...], head_ref[...], 1, 0))
    exp_ref[...] = exp_logits
    groups = exp_logits[:, :128]
    for start in range(128, exp_logits.shape[1], 128):
        groups = groups + exp_logits[:, start : start + 128]
    sums = lax.dot_general(
        jnp.ones((8, 128), f32), groups, (((1,), (1,)), ((), ())), precision=lax.Precision.HIGHEST, preferred_element_type=f32
    )
    sum_ref[...] = sums[:1]


def spread(rows):
    ones = jnp.ones((rows.shape[0], 128), f32)
    return lax.dot_general(
        rows, ones, (((0,), (0,)), ((), ())), precision=lax.Precision.HIGHEST, preferred_element_type=f32
    )


def dlogit_rows(first, exp_ref, totals_ref, code_ref, mask_ref, rows):
    window = pl.ds(first, rows)
    total, code, weight = (spread(ref[:, window]) for ref in (totals_ref, code_ref, mask_ref))
    scale = weight / total
    parts = []
    for start in range(0, exp_ref.shape[1], 128):
        columns = (lax.broadcasted_iota(jnp.int32, (rows, 128), 1) + start).astype(f32)
        onehot = jnp.where(columns == code, weight, 0.0)
        parts.append((scale * exp_ref[window, start : start + 128] - onehot).astype(bf16))
    return jnp.concatenate(parts, axis=1)


def sent_grad(half_ref, exp_ref, totals_ref, code_ref, mask_ref, head_ref, out_ref):
    rows = out_ref.shape[0]
    start = pl.multiple_of(half_ref[0] * rows, rows)
    dlogit = dlogit_rows(start, exp_ref, totals_ref, code_ref, mask_ref, rows)
    out_ref[...] = dot(dlogit, head_ref[...], 1, 1).astype(out_ref.dtype)


def copy_out(source_ref, target_hbm, sems):
    copies = [pltpu.make_async_copy(source_ref.at[i], target_hbm.at[i], sems.at[i]) for i in range(source_ref.shape[0])]
    for copy in copies:
        copy.start()
    return copies


def kept_grad(
    half_ref, exp_ref, totals_ref, code_ref, mask_ref, head_ref, normed_ref,
    out_ref, late_ref, early_hbm, dlogit_ref, early_ref, sems,
):
    dlogit_ref[...] = dlogit_rows(0, exp_ref, totals_ref, code_ref, mask_ref, exp_ref.shape[0])
    grad = dot(normed_ref[...], dlogit_ref[...], 0, 0).astype(bf16)
    part = grad.shape[1]
    for i in range(BLOCKS - PROJ_BLOCKS):
        top, bottom = grad[16 * i : 16 * i + 8], grad[16 * i + 8 : 16 * i + 16]
        if PROJ_BLOCKS + i < LATE_BLOCKS:
            late_ref[i, :, :part] = top
            late_ref[i, :, part:] = bottom
        else:
            _, yl, xh, zh, zl = place(PROJ_BLOCKS + i)
            row = 8 * (xh * 6 + zh)
            early_ref[2 * yl + zl, row : row + 8, :part] = top
            early_ref[2 * yl + zl, row : row + 8, part:] = bottom
    copies = copy_out(early_ref, early_hbm, sems)
    rows = out_ref.shape[0]
    start = pl.multiple_of(half_ref[0] * rows, rows)
    out_ref[...] = dot(dlogit_ref[pl.ds(start, rows), :], head_ref[...], 1, 1)
    for copy in copies:
        copy.wait()


def grad_blocks(hidden_ref, grad_ref, head_ref, out_hbm, out_ref, sems):
    step = 16
    for first in range(0, LATE_BLOCKS, step):
        if first < PROJ_BLOCKS:
            part = dot(hidden_ref[:, 8 * first : 8 * (first + step)], grad_ref[...], 0, 0).astype(bf16)
        for i in range(step):
            yh, yl, xh, zh, zl = place(first + i)
            row = 8 * (zh * 3 + yh)
            block = part[8 * i : 8 * i + 8] if first < PROJ_BLOCKS else head_ref[i]
            out_ref[(xh * 2 + yl) * 2 + zl, row : row + 8, :] = block
    for copy in copy_out(out_ref, out_hbm, sems):
        copy.wait()


def early_sum(half_ref, pieces_ref, sent_ref, kept_ref):
    rows = sent_ref.shape[0]
    mine = pl.ds(pl.multiple_of(half_ref[0] * rows, rows), rows)
    other = pl.ds(pl.multiple_of((1 - half_ref[0]) * rows, rows), rows)
    sent_ref[...] = add_up(pieces_ref.at[:, other]).astype(sent_ref.dtype)
    kept_ref[...] = add_up(pieces_ref.at[:, mine])


def chip_sum(kept_ref, other_ref, out_ref):
    out_ref[...] = (kept_ref[...] + other_ref[...].astype(f32)).astype(out_ref.dtype)


def near_sum(pieces_ref, kept_ref, other_ref, out_ref):
    for zh in range(6):
        window = slice(24 * zh, 24 * zh + 24)
        out_ref[32 * zh : 32 * zh + 24] = add_up(pieces_ref.at[:, window]).astype(out_ref.dtype)
        window = slice(8 * zh, 8 * zh + 8)
        early = kept_ref[window] + other_ref[window].astype(f32)
        out_ref[32 * zh + 24 : 32 * zh + 32] = early.astype(out_ref.dtype)


def far_sum(is_proj_ref, pieces_ref, out_ref):
    total = add_up(pieces_ref)
    rows, part = total.shape[0], out_ref.shape[1]

    @pl.when(is_proj_ref[0] == 1)
    def _():
        for row in range(rows):
            out_ref[2 * row : 2 * row + 1, :] = total[row : row + 1, :part]
            out_ref[2 * row + 1 : 2 * row + 2, :] = total[row : row + 1, part:]

    @pl.when(is_proj_ref[0] == 0)
    def _():
        out_ref[:rows, :] = total[:, :part]
        out_ref[rows:, :] = total[:, part:]


def in_vmem(kernel, outs, n_in, scalars=0):
    vmem = pl.BlockSpec(memory_space=pltpu.VMEM)
    smem = pl.BlockSpec(memory_space=pltpu.SMEM)
    return pl.pallas_call(
        kernel,
        out_shape=outs,
        in_specs=[smem] * scalars + [vmem] * n_in,
        out_specs=jax.tree.map(lambda _: vmem, outs),
        compiler_params=pltpu.CompilerParams(vmem_limit_bytes=VMEM_BYTES),
    )


def shape(dims, dtype):
    return jax.ShapeDtypeStruct(dims, dtype)


def local(hidden, in_proj, norm_gain, head_weight, code_ids, stream_mask):
    frames, width = hidden.shape[0], in_proj.shape[1]
    vocab_part = head_weight.shape[1]
    half = frames // 2
    tp = lax.axis_index(TP)
    gain = norm_gain[None, :]
    mine = lax.axis_index("core").reshape(1)
    other = 1 - mine
    code = (code_ids - tp * vocab_part).astype(f32)[None, :]
    mask = stream_mask.astype(f32)[None, :]

    steps, inner = 4, hidden.shape[1]
    sent, kept = pl.pallas_call(
        streamed_product,
        out_shape=[shape((half, width), bf16), shape((half, width), f32)],
        in_specs=[pl.BlockSpec(memory_space=pltpu.SMEM)] + [pl.BlockSpec(memory_space=pltpu.HBM)] * 2,
        out_specs=[pl.BlockSpec(memory_space=pltpu.VMEM)] * 2,
        scratch_shapes=[
            pltpu.VMEM((frames, inner), bf16),
            pltpu.VMEM((steps, inner // steps, width), bf16),
            pltpu.SemaphoreType.DMA((steps + 1,)),
        ],
        compiler_params=pltpu.CompilerParams(vmem_limit_bytes=VMEM_BYTES),
    )(mine, *(pltpu.with_memory_space_constraint(array, pltpu.HBM) for array in (hidden, in_proj)))
    chip = in_vmem(chip_sum, shape((half, width), bf16), 2)(kept, lax.ppermute(sent, "core", SWAP))
    x = add_up(lax.all_gather(chip, "xl"))
    inv_rms = lax.rsqrt(jnp.mean(x * x, axis=1, keepdims=True) + norm_eps)
    unit_rows = x * inv_rms
    normed = lax.all_gather((unit_rows * gain).astype(bf16), "core", tiled=True)

    exp_logits, sums = in_vmem(
        exp_rows, [shape((frames, vocab_part), f32), shape((1, frames), f32)], 2
    )(normed, head_weight)
    totals = lax.all_gather(sums, TP, tiled=True)

    rest = (exp_logits, totals, code, mask, head_weight)
    sent = in_vmem(sent_grad, shape((half, width), bf16), 5, 1)(other, *rest)
    exp_logits, sent = lax.optimization_barrier((exp_logits, sent))
    rest = (exp_logits, *rest[1:])
    vmem = pl.BlockSpec(memory_space=pltpu.VMEM)
    hbm = pl.BlockSpec(memory_space=pltpu.HBM)
    kept, late_head, early = pl.pallas_call(
        kept_grad,
        out_shape=[
            shape((half, width), f32),
            shape((LATE_BLOCKS - PROJ_BLOCKS, 8, width), bf16),
            shape((4, 96, width), bf16),
        ],
        in_specs=[pl.BlockSpec(memory_space=pltpu.SMEM)] + [vmem] * 6,
        out_specs=[vmem, vmem, hbm],
        scratch_shapes=[
            pltpu.VMEM((frames, vocab_part), bf16),
            pltpu.VMEM((4, 96, width), bf16),
            pltpu.SemaphoreType.DMA((4,)),
        ],
        compiler_params=pltpu.CompilerParams(vmem_limit_bytes=VMEM_BYTES),
    )(mine, *rest, normed)
    early, swapped = lax.optimization_barrier((early, lax.ppermute(sent, "core", SWAP)))
    early = lax.all_to_all(early, EARLY, 0, 0)
    chip = in_vmem(chip_sum, shape((half, width), bf16), 2)(kept, swapped)
    scaled_grad = add_up(lax.all_gather(chip, "xl")) * gain
    centred = scaled_grad - unit_rows * jnp.mean(scaled_grad * unit_rows, axis=1, keepdims=True)
    row_grad = lax.all_gather((inv_rms * centred).astype(bf16), "core", tiled=True)

    blocks = pl.pallas_call(
        grad_blocks,
        out_shape=shape((N_NEAR, LATE_BLOCKS, width), bf16),
        in_specs=[vmem] * 3,
        out_specs=hbm,
        scratch_shapes=[
            pltpu.VMEM((N_NEAR, LATE_BLOCKS, width), bf16),
            pltpu.SemaphoreType.DMA((N_NEAR,)),
        ],
        compiler_params=pltpu.CompilerParams(vmem_limit_bytes=VMEM_BYTES),
    )(hidden, row_grad, late_head)
    early_out = [shape((48, width), bf16), shape((48, width), f32)]
    early_sent, early_kept = in_vmem(early_sum, early_out, 1, 1)(lax.axis_index("xh").reshape(1), early)
    blocks, early_sent = lax.optimization_barrier((blocks, early_sent))
    pieces = lax.all_to_all(blocks, NEAR, 0, 0)
    early_other = lax.ppermute(early_sent, "xh", SWAP)
    near = in_vmem(near_sum, shape((N_FAR * 8, width), bf16), 3)(
        pieces, early_kept, early_other
    )
    far = lax.all_to_all(near.reshape(N_FAR, 8, width), FAR, 0, 0)
    is_proj = (lax.axis_index(SEQ) < PROJ_BLOCKS).astype(jnp.int32).reshape(1)
    weight_grads = in_vmem(far_sum, shape((16, vocab_part), f32), 1, 1)(is_proj, far)

    hidden_grad = pl.pallas_call(
        hidden_rows,
        out_shape=shape((frames, inner), bf16),
        in_specs=[pl.BlockSpec(memory_space=pltpu.VMEM), pl.BlockSpec(memory_space=pltpu.HBM)],
        out_specs=pl.BlockSpec(memory_space=pltpu.VMEM),
        scratch_shapes=[
            pltpu.VMEM((steps, inner // steps, width), bf16),
            pltpu.SemaphoreType.DMA((steps,)),
        ],
        compiler_params=pltpu.CompilerParams(vmem_limit_bytes=VMEM_BYTES),
        cost_estimate=pl.CostEstimate(
            flops=2 * frames * inner * width, transcendentals=0, bytes_accessed=2 * width * (inner + 2 * frames)
        ),
    )(row_grad, pltpu.with_memory_space_constraint(in_proj, pltpu.HBM))
    return (hidden_grad, weight_grads[None])


def solution(mesh):
    fine = Mesh(mesh.devices.reshape(SIZES), AXES)
    in_specs = (P(SEQ, TP), P(TP, None), P(), P(None, TP), P(SEQ), P(SEQ))
    out_specs = (P(SEQ, TP), P(TP, SEQ, None))
    return jax.shard_map(local, mesh=fine, in_specs=in_specs, out_specs=out_specs, check_vma=False)
```

```python
import jax
import jax.numpy as jnp
from jax import lax
from jax.experimental import pallas as pl
from jax.experimental.pallas import tpu as pltpu
from jax.sharding import Mesh
from jax.sharding import PartitionSpec as P

norm_eps = 1e-05
loss_scale = 16.0

AXES = ("yh", "yl", "xh", "zh", "zl", "xl", "core")
SIZES = (4, 2, 2, 6, 2, 2, 2)
SEQ = ("yh", "yl", "xh", "zh", "zl")
TP = ("xl", "core")
NEAR = ("xh", "yl", "zl")
FAR = ("zh", "yh")
N_NEAR = 8
N_FAR = 24
BLOCKS = 192
PROJ_BLOCKS = 128
LATE_BLOCKS = 144
EARLY = ("yl", "zl")
VMEM_BYTES = 20 << 20
SWAP = [(0, 1), (1, 0)]
f32 = jnp.float32
bf16 = jnp.bfloat16


def dot(a, b, ca, cb):
    return lax.dot_general(a, b, (((ca,), (cb,)), ((), ())), preferred_element_type=f32)


def add_up(pieces):
    total = pieces[0].astype(f32)
    for i in range(1, pieces.shape[0]):
        total = total + pieces[i].astype(f32)
    return total


def place(block):
    y, x, z = block // 24, block // 12 % 2, block % 12
    return y // 2, y % 2, x, z // 2, z % 2


def streamed_product(half_ref, a_hbm, b_hbm, sent_ref, kept_ref, a_ref, b_ref, sems):
    rows, steps, depth = sent_ref.shape[0], b_ref.shape[0], b_ref.shape[1]
    copies = [pltpu.make_async_copy(a_hbm, a_ref, sems.at[steps])]
    for i in range(steps):
        copies.append(pltpu.make_async_copy(b_hbm.at[i * depth : (i + 1) * depth, :], b_ref.at[i], sems.at[i]))
    for copy in copies:
        copy.start()
    copies[0].wait()
    mine = pl.ds(pl.multiple_of(half_ref[0] * rows, rows), rows)
    other = pl.ds(pl.multiple_of((1 - half_ref[0]) * rows, rows), rows)
    sent = kept = None
    for i in range(steps):
        copies[1 + i].wait()
        columns = slice(i * depth, (i + 1) * depth)
        sent_part = dot(a_ref[other, columns], b_ref[i], 1, 0)
        kept_part = dot(a_ref[mine, columns], b_ref[i], 1, 0)
        sent = sent_part if i == 0 else sent + sent_part
        kept = kept_part if i == 0 else kept + kept_part
    sent_ref[...] = sent.astype(sent_ref.dtype)
    kept_ref[...] = kept


def hidden_rows(grad_ref, b_hbm, out_ref, b_ref, sems):
    steps, depth = b_ref.shape[0], b_ref.shape[1]
    copies = [
        pltpu.make_async_copy(b_hbm.at[i * depth : (i + 1) * depth, :], b_ref.at[i], sems.at[i]) for i in range(steps)
    ]
    for copy in copies:
        copy.start()
    for i in range(steps):
        copies[i].wait()
        part = loss_scale * dot(grad_ref[...], b_ref[i], 1, 1)
        out_ref[:, i * depth : (i + 1) * depth] = part.astype(out_ref.dtype)


def exp_rows(normed_ref, head_ref, exp_ref, sum_ref):
    exp_logits = jnp.exp(dot(normed_ref[...], head_ref[...], 1, 0))
    exp_ref[...] = exp_logits
    groups = exp_logits[:, :128]
    for start in range(128, exp_logits.shape[1], 128):
        groups = groups + exp_logits[:, start : start + 128]
    sums = lax.dot_general(
        jnp.ones((8, 128), f32), groups, (((1,), (1,)), ((), ())), precision=lax.Precision.HIGHEST, preferred_element_type=f32
    )
    sum_ref[...] = sums[:1]


def spread(rows):
    ones = jnp.ones((rows.shape[0], 128), f32)
    return lax.dot_general(
        rows, ones, (((0,), (0,)), ((), ())), precision=lax.Precision.HIGHEST, preferred_element_type=f32
    )


def dlogit_rows(first, column, exp_ref, totals_ref, code_ref, mask_ref, rows):
    window = pl.ds(first, rows)
    total, code, weight = (spread(ref[:, window].astype(f32)) for ref in (totals_ref, code_ref, mask_ref))
    scale = weight / total
    parts = []
    for start in range(0, exp_ref.shape[1], 128):
        columns = (lax.broadcasted_iota(jnp.int32, (rows, 128), 1) + (column + start)).astype(f32)
        onehot = jnp.where(columns == code, weight, 0.0)
        parts.append((scale * exp_ref[window, start : start + 128] - onehot).astype(bf16))
    return jnp.concatenate(parts, axis=1)


def sent_grad(half_ref, column_ref, exp_ref, totals_ref, code_ref, mask_ref, head_ref, out_ref):
    rows = out_ref.shape[0]
    start = pl.multiple_of(half_ref[0] * rows, rows)
    dlogit = dlogit_rows(start, column_ref[0], exp_ref, totals_ref, code_ref, mask_ref, rows)
    out_ref[...] = dot(dlogit, head_ref[...], 1, 1).astype(out_ref.dtype)


def copy_out(source_ref, target_hbm, sems):
    copies = [pltpu.make_async_copy(source_ref.at[i], target_hbm.at[i], sems.at[i]) for i in range(source_ref.shape[0])]
    for copy in copies:
        copy.start()
    return copies


def kept_grad(
    half_ref, column_ref, exp_ref, totals_ref, code_ref, mask_ref, head_ref, normed_ref,
    out_ref, late_ref, early_hbm, dlogit_ref, early_ref, sems,
):
    dlogit_ref[...] = dlogit_rows(0, column_ref[0], exp_ref, totals_ref, code_ref, mask_ref, exp_ref.shape[0])
    grad = dot(normed_ref[...], dlogit_ref[...], 0, 0).astype(bf16)
    part = grad.shape[1]
    for i in range(BLOCKS - PROJ_BLOCKS):
        top, bottom = grad[16 * i : 16 * i + 8], grad[16 * i + 8 : 16 * i + 16]
        if PROJ_BLOCKS + i < LATE_BLOCKS:
            late_ref[i, :, :part] = top
            late_ref[i, :, part:] = bottom
        else:
            _, yl, xh, zh, zl = place(PROJ_BLOCKS + i)
            row = 8 * (xh * 6 + zh)
            early_ref[2 * yl + zl, row : row + 8, :part] = top
            early_ref[2 * yl + zl, row : row + 8, part:] = bottom
    copies = copy_out(early_ref, early_hbm, sems)
    rows = out_ref.shape[0]
    start = pl.multiple_of(half_ref[0] * rows, rows)
    out_ref[...] = dot(dlogit_ref[pl.ds(start, rows), :], head_ref[...], 1, 1)
    for copy in copies:
        copy.wait()


def grad_blocks(hidden_ref, grad_ref, head_ref, out_hbm, out_ref, sems):
    step = 16
    for first in range(0, LATE_BLOCKS, step):
        if first < PROJ_BLOCKS:
            part = dot(hidden_ref[:, 8 * first : 8 * (first + step)], grad_ref[...], 0, 0).astype(bf16)
        for i in range(step):
            yh, yl, xh, zh, zl = place(first + i)
            row = 8 * (zh * 3 + yh)
            block = part[8 * i : 8 * i + 8] if first < PROJ_BLOCKS else head_ref[i]
            out_ref[(xh * 2 + yl) * 2 + zl, row : row + 8, :] = block
    for copy in copy_out(out_ref, out_hbm, sems):
        copy.wait()


def early_sum(half_ref, pieces_ref, sent_ref, kept_ref):
    rows = sent_ref.shape[0]
    mine = pl.ds(pl.multiple_of(half_ref[0] * rows, rows), rows)
    other = pl.ds(pl.multiple_of((1 - half_ref[0]) * rows, rows), rows)
    sent_ref[...] = add_up(pieces_ref.at[:, other]).astype(sent_ref.dtype)
    kept_ref[...] = add_up(pieces_ref.at[:, mine])


def chip_sum_of(half_ref, kept_ref, both_ref, out_ref):
    out_ref[...] = (kept_ref[...] + both_ref[1 - half_ref[0]].astype(f32)).astype(out_ref.dtype)


def chip_sum(kept_ref, other_ref, out_ref):
    out_ref[...] = (kept_ref[...] + other_ref[...].astype(f32)).astype(out_ref.dtype)


def near_sum(pieces_ref, kept_ref, other_ref, out_ref):
    for zh in range(6):
        window = slice(24 * zh, 24 * zh + 24)
        out_ref[32 * zh : 32 * zh + 24] = add_up(pieces_ref.at[:, window]).astype(out_ref.dtype)
        window = slice(8 * zh, 8 * zh + 8)
        early = kept_ref[window] + other_ref[window].astype(f32)
        out_ref[32 * zh + 24 : 32 * zh + 32] = early.astype(out_ref.dtype)


def far_sum(is_proj_ref, pieces_ref, out_ref):
    total = add_up(pieces_ref)
    rows, part = total.shape[0], out_ref.shape[1]

    @pl.when(is_proj_ref[0] == 1)
    def _():
        for row in range(rows):
            out_ref[2 * row : 2 * row + 1, :] = total[row : row + 1, :part]
            out_ref[2 * row + 1 : 2 * row + 2, :] = total[row : row + 1, part:]

    @pl.when(is_proj_ref[0] == 0)
    def _():
        out_ref[:rows, :] = total[:, :part]
        out_ref[rows:, :] = total[:, part:]


def in_vmem(kernel, outs, n_in, scalars=0):
    vmem = pl.BlockSpec(memory_space=pltpu.VMEM)
    smem = pl.BlockSpec(memory_space=pltpu.SMEM)
    return pl.pallas_call(
        kernel,
        out_shape=outs,
        in_specs=[smem] * scalars + [vmem] * n_in,
        out_specs=jax.tree.map(lambda _: vmem, outs),
        compiler_params=pltpu.CompilerParams(vmem_limit_bytes=VMEM_BYTES),
    )


def shape(dims, dtype):
    return jax.ShapeDtypeStruct(dims, dtype)


def local(hidden, in_proj, norm_gain, head_weight, code_ids, stream_mask):
    frames, width = hidden.shape[0], in_proj.shape[1]
    vocab_part = head_weight.shape[1]
    half = frames // 2
    tp = lax.axis_index(TP)
    gain = norm_gain[None, :]
    mine = lax.axis_index("core").reshape(1)
    other = 1 - mine
    code, mask = code_ids[None, :], stream_mask[None, :]
    first_column = (tp * vocab_part).reshape(1)

    steps, inner = 8, hidden.shape[1]
    sent, kept = pl.pallas_call(
        streamed_product,
        out_shape=[shape((half, width), bf16), shape((half, width), f32)],
        in_specs=[pl.BlockSpec(memory_space=pltpu.SMEM)] + [pl.BlockSpec(memory_space=pltpu.HBM)] * 2,
        out_specs=[pl.BlockSpec(memory_space=pltpu.VMEM)] * 2,
        scratch_shapes=[
            pltpu.VMEM((frames, inner), bf16),
            pltpu.VMEM((steps, inner // steps, width), bf16),
            pltpu.SemaphoreType.DMA((steps + 1,)),
        ],
        compiler_params=pltpu.CompilerParams(vmem_limit_bytes=VMEM_BYTES),
    )(mine, *(pltpu.with_memory_space_constraint(array, pltpu.HBM) for array in (hidden, in_proj)))
    chip = in_vmem(chip_sum_of, shape((half, width), bf16), 2, 1)(mine, kept, lax.all_gather(sent, "core"))
    x = add_up(lax.all_gather(chip, "xl"))
    inv_rms = lax.rsqrt(jnp.mean(x * x, axis=1, keepdims=True) + norm_eps)
    unit_rows = x * inv_rms
    normed = lax.all_gather((unit_rows * gain).astype(bf16), "core", tiled=True)

    exp_logits, sums = in_vmem(
        exp_rows, [shape((frames, vocab_part), f32), shape((1, frames), f32)], 2
    )(normed, head_weight)
    totals = lax.all_gather(sums, TP, tiled=True)

    rest = (exp_logits, totals, code, mask, head_weight)
    sent = in_vmem(sent_grad, shape((half, width), bf16), 5, 2)(other, first_column, *rest)
    exp_logits, sent = lax.optimization_barrier((exp_logits, sent))
    rest = (exp_logits, *rest[1:])
    vmem = pl.BlockSpec(memory_space=pltpu.VMEM)
    hbm = pl.BlockSpec(memory_space=pltpu.HBM)
    kept, late_head, early = pl.pallas_call(
        kept_grad,
        out_shape=[
            shape((half, width), f32),
            shape((LATE_BLOCKS - PROJ_BLOCKS, 8, width), bf16),
            shape((4, 96, width), bf16),
        ],
        in_specs=[pl.BlockSpec(memory_space=pltpu.SMEM)] * 2 + [vmem] * 6,
        out_specs=[vmem, vmem, hbm],
        scratch_shapes=[
            pltpu.VMEM((frames, vocab_part), bf16),
            pltpu.VMEM((4, 96, width), bf16),
            pltpu.SemaphoreType.DMA((4,)),
        ],
        compiler_params=pltpu.CompilerParams(vmem_limit_bytes=VMEM_BYTES),
    )(mine, first_column, *rest, normed)
    early, swapped = lax.optimization_barrier((early, lax.ppermute(sent, "core", SWAP)))
    early = lax.all_to_all(early, EARLY, 0, 0)
    chip = in_vmem(chip_sum, shape((half, width), bf16), 2)(kept, swapped)
    scaled_grad = add_up(lax.all_gather(chip, "xl")) * gain
    centred = scaled_grad - unit_rows * jnp.mean(scaled_grad * unit_rows, axis=1, keepdims=True)
    row_grad = lax.all_gather((inv_rms * centred).astype(bf16), "core", tiled=True)

    blocks = pl.pallas_call(
        grad_blocks,
        out_shape=shape((N_NEAR, LATE_BLOCKS, width), bf16),
        in_specs=[vmem] * 3,
        out_specs=hbm,
        scratch_shapes=[
            pltpu.VMEM((N_NEAR, LATE_BLOCKS, width), bf16),
            pltpu.SemaphoreType.DMA((N_NEAR,)),
        ],
        compiler_params=pltpu.CompilerParams(vmem_limit_bytes=VMEM_BYTES),
    )(hidden, row_grad, late_head)
    early_out = [shape((48, width), bf16), shape((48, width), f32)]
    early_sent, early_kept = in_vmem(early_sum, early_out, 1, 1)(lax.axis_index("xh").reshape(1), early)
    blocks, early_sent = lax.optimization_barrier((blocks, early_sent))
    pieces = lax.all_to_all(blocks, NEAR, 0, 0)
    early_other = lax.ppermute(early_sent, "xh", SWAP)
    near = in_vmem(near_sum, shape((N_FAR * 8, width), bf16), 3)(
        pieces, early_kept, early_other
    )
    far = lax.all_to_all(near.reshape(N_FAR, 8, width), FAR, 0, 0)
    is_proj = (lax.axis_index(SEQ) < PROJ_BLOCKS).astype(jnp.int32).reshape(1)
    weight_grads = in_vmem(far_sum, shape((16, vocab_part), f32), 1, 1)(is_proj, far)

    hidden_grad = pl.pallas_call(
        hidden_rows,
        out_shape=shape((frames, inner), bf16),
        in_specs=[pl.BlockSpec(memory_space=pltpu.VMEM), pl.BlockSpec(memory_space=pltpu.HBM)],
        out_specs=pl.BlockSpec(memory_space=pltpu.VMEM),
        scratch_shapes=[
            pltpu.VMEM((steps, inner // steps, width), bf16),
            pltpu.SemaphoreType.DMA((steps,)),
        ],
        compiler_params=pltpu.CompilerParams(vmem_limit_bytes=VMEM_BYTES),
        cost_estimate=pl.CostEstimate(
            flops=2 * frames * inner * width, transcendentals=0, bytes_accessed=2 * width * (inner + 2 * frames)
        ),
    )(row_grad, pltpu.with_memory_space_constraint(in_proj, pltpu.HBM))
    return (hidden_grad, weight_grads[None])


def solution(mesh):
    fine = Mesh(mesh.devices.reshape(SIZES), AXES)
    in_specs = (P(SEQ, TP), P(TP, None), P(), P(None, TP), P(SEQ), P(SEQ))
    out_specs = (P(SEQ, TP), P(TP, SEQ, None))
    return jax.shard_map(local, mesh=fine, in_specs=in_specs, out_specs=out_specs, check_vma=False)
```

```python
import jax
import jax.numpy as jnp
from jax import lax
from jax.experimental import pallas as pl
from jax.experimental.pallas import tpu as pltpu
from jax.sharding import Mesh
from jax.sharding import PartitionSpec as P

norm_eps = 1e-05
loss_scale = 16.0

AXES = ("yh", "yl", "xh", "zh", "zl", "xl", "core")
SIZES = (4, 2, 2, 6, 2, 2, 2)
SEQ = ("yh", "yl", "xh", "zh", "zl")
TP = ("xl", "core")
NEAR = ("xh", "yl", "zl")
FAR = ("zh", "yh")
N_NEAR = 8
N_FAR = 24
BLOCKS = 192
PROJ_BLOCKS = 128
LATE_BLOCKS = 144
EARLY = ("yl", "zl")
VMEM_BYTES = 20 << 20
SWAP = [(0, 1), (1, 0)]
f32 = jnp.float32
bf16 = jnp.bfloat16


def dot(a, b, ca, cb):
    return lax.dot_general(a, b, (((ca,), (cb,)), ((), ())), preferred_element_type=f32)


def add_up(pieces):
    total = pieces[0].astype(f32)
    for i in range(1, pieces.shape[0]):
        total = total + pieces[i].astype(f32)
    return total


def place(block):
    y, x, z = block // 24, block // 12 % 2, block % 12
    return y // 2, y % 2, x, z // 2, z % 2


def streamed_product(half_ref, a_hbm, b_hbm, sent_ref, kept_ref, a_ref, b_ref, sems):
    rows, steps, depth = sent_ref.shape[0], b_ref.shape[0], b_ref.shape[1]
    copies = [pltpu.make_async_copy(a_hbm, a_ref, sems.at[steps])]
    for i in range(steps):
        copies.append(pltpu.make_async_copy(b_hbm.at[i * depth : (i + 1) * depth, :], b_ref.at[i], sems.at[i]))
    for copy in copies:
        copy.start()
    copies[0].wait()
    mine = pl.ds(pl.multiple_of(half_ref[0] * rows, rows), rows)
    other = pl.ds(pl.multiple_of((1 - half_ref[0]) * rows, rows), rows)
    sent = kept = None
    for i in range(steps):
        copies[1 + i].wait()
        columns = slice(i * depth, (i + 1) * depth)
        sent_part = dot(a_ref[other, columns], b_ref[i], 1, 0)
        kept_part = dot(a_ref[mine, columns], b_ref[i], 1, 0)
        sent = sent_part if i == 0 else sent + sent_part
        kept = kept_part if i == 0 else kept + kept_part
    sent_ref[...] = sent.astype(sent_ref.dtype)
    kept_ref[...] = kept


def hidden_rows(grad_ref, b_hbm, out_ref, b_ref, sems):
    steps, depth = b_ref.shape[0], b_ref.shape[1]
    copies = [
        pltpu.make_async_copy(b_hbm.at[i * depth : (i + 1) * depth, :], b_ref.at[i], sems.at[i]) for i in range(steps)
    ]
    for copy in copies:
        copy.start()
    for i in range(steps):
        copies[i].wait()
        part = loss_scale * dot(grad_ref[...], b_ref[i], 1, 1)
        out_ref[:, i * depth : (i + 1) * depth] = part.astype(out_ref.dtype)


def exp_rows(normed_ref, head_ref, exp_ref, sum_ref):
    exp_logits = jnp.exp(dot(normed_ref[...], head_ref[...], 1, 0))
    exp_ref[...] = exp_logits
    groups = exp_logits[:, :128]
    for start in range(128, exp_logits.shape[1], 128):
        groups = groups + exp_logits[:, start : start + 128]
    sums = lax.dot_general(
        jnp.ones((8, 128), f32), groups, (((1,), (1,)), ((), ())), precision=lax.Precision.HIGHEST, preferred_element_type=f32
    )
    sum_ref[...] = sums[:1]


def spread(rows):
    ones = jnp.ones((rows.shape[0], 128), f32)
    return lax.dot_general(
        rows, ones, (((0,), (0,)), ((), ())), precision=lax.Precision.HIGHEST, preferred_element_type=f32
    )


def dlogit_rows(first, column, exp_ref, totals_ref, code_ref, mask_ref, rows):
    window = pl.ds(first, rows)
    total, code, weight = (spread(ref[:, window].astype(f32)) for ref in (totals_ref, code_ref, mask_ref))
    scale = weight / total
    parts = []
    for start in range(0, exp_ref.shape[1], 128):
        columns = (lax.broadcasted_iota(jnp.int32, (rows, 128), 1) + (column + start)).astype(f32)
        onehot = jnp.where(columns == code, weight, 0.0)
        parts.append((scale * exp_ref[window, start : start + 128] - onehot).astype(bf16))
    return jnp.concatenate(parts, axis=1)


def sent_grad(half_ref, column_ref, exp_ref, totals_ref, code_ref, mask_ref, head_ref, out_ref):
    rows = out_ref.shape[0]
    start = pl.multiple_of(half_ref[0] * rows, rows)
    dlogit = dlogit_rows(start, column_ref[0], exp_ref, totals_ref, code_ref, mask_ref, rows)
    out_ref[...] = dot(dlogit, head_ref[...], 1, 1).astype(out_ref.dtype)


def copy_out(source_ref, target_hbm, sems):
    copies = [pltpu.make_async_copy(source_ref.at[i], target_hbm.at[i], sems.at[i]) for i in range(source_ref.shape[0])]
    for copy in copies:
        copy.start()
    return copies


def kept_grad(
    half_ref, column_ref, exp_ref, totals_ref, code_ref, mask_ref, head_ref, normed_ref,
    out_ref, late_ref, early_hbm, dlogit_ref, early_ref, sems,
):
    dlogit_ref[...] = dlogit_rows(0, column_ref[0], exp_ref, totals_ref, code_ref, mask_ref, exp_ref.shape[0])
    grad = dot(normed_ref[...], dlogit_ref[...], 0, 0).astype(bf16)
    part = grad.shape[1]
    for i in range(BLOCKS - PROJ_BLOCKS):
        top, bottom = grad[16 * i : 16 * i + 8], grad[16 * i + 8 : 16 * i + 16]
        if PROJ_BLOCKS + i < LATE_BLOCKS:
            late_ref[i, :, :part] = top
            late_ref[i, :, part:] = bottom
        else:
            _, yl, xh, zh, zl = place(PROJ_BLOCKS + i)
            row = 8 * (xh * 6 + zh)
            early_ref[2 * yl + zl, row : row + 8, :part] = top
            early_ref[2 * yl + zl, row : row + 8, part:] = bottom
    copies = copy_out(early_ref, early_hbm, sems)
    rows = out_ref.shape[0]
    start = pl.multiple_of(half_ref[0] * rows, rows)
    out_ref[...] = dot(dlogit_ref[pl.ds(start, rows), :], head_ref[...], 1, 1)
    for copy in copies:
        copy.wait()


def grad_blocks(hidden_ref, grad_ref, head_ref, out_hbm, out_ref, sems):
    step = 16
    for first in range(0, LATE_BLOCKS, step):
        if first < PROJ_BLOCKS:
            part = dot(hidden_ref[:, 8 * first : 8 * (first + step)], grad_ref[...], 0, 0).astype(bf16)
        for i in range(step):
            yh, yl, xh, zh, zl = place(first + i)
            row = 8 * (zh * 3 + yh)
            block = part[8 * i : 8 * i + 8] if first < PROJ_BLOCKS else head_ref[i]
            out_ref[(xh * 2 + yl) * 2 + zl, row : row + 8, :] = block
    for copy in copy_out(out_ref, out_hbm, sems):
        copy.wait()


def norm_back(x_ref, grad_ref, gain_ref, out_ref):
    x, grad = add_up(x_ref), add_up(grad_ref)
    inv_rms = lax.rsqrt(jnp.mean(x * x, axis=1, keepdims=True) + norm_eps)
    unit_rows = x * inv_rms
    scaled_grad = grad * gain_ref[...]
    centred = scaled_grad - unit_rows * jnp.mean(scaled_grad * unit_rows, axis=1, keepdims=True)
    out_ref[...] = (inv_rms * centred).astype(out_ref.dtype)


def early_sum(half_ref, pieces_ref, sent_ref, kept_ref):
    rows = sent_ref.shape[0]
    mine = pl.ds(pl.multiple_of(half_ref[0] * rows, rows), rows)
    other = pl.ds(pl.multiple_of((1 - half_ref[0]) * rows, rows), rows)
    sent_ref[...] = add_up(pieces_ref.at[:, other]).astype(sent_ref.dtype)
    kept_ref[...] = add_up(pieces_ref.at[:, mine])


def chip_sum_of(half_ref, kept_ref, both_ref, out_ref):
    out_ref[...] = (kept_ref[...] + both_ref[1 - half_ref[0]].astype(f32)).astype(out_ref.dtype)


def chip_sum(kept_ref, other_ref, out_ref):
    out_ref[...] = (kept_ref[...] + other_ref[...].astype(f32)).astype(out_ref.dtype)


def near_sum(pieces_ref, kept_ref, other_ref, out_ref):
    for zh in range(6):
        window = slice(24 * zh, 24 * zh + 24)
        out_ref[32 * zh : 32 * zh + 24] = add_up(pieces_ref.at[:, window]).astype(out_ref.dtype)
        window = slice(8 * zh, 8 * zh + 8)
        early = kept_ref[window] + other_ref[window].astype(f32)
        out_ref[32 * zh + 24 : 32 * zh + 32] = early.astype(out_ref.dtype)


def far_sum(is_proj_ref, pieces_ref, out_ref):
    total = add_up(pieces_ref)
    rows, part = total.shape[0], out_ref.shape[1]

    @pl.when(is_proj_ref[0] == 1)
    def _():
        for row in range(rows):
            out_ref[2 * row : 2 * row + 1, :] = total[row : row + 1, :part]
            out_ref[2 * row + 1 : 2 * row + 2, :] = total[row : row + 1, part:]

    @pl.when(is_proj_ref[0] == 0)
    def _():
        out_ref[:rows, :] = total[:, :part]
        out_ref[rows:, :] = total[:, part:]


def in_vmem(kernel, outs, n_in, scalars=0):
    vmem = pl.BlockSpec(memory_space=pltpu.VMEM)
    smem = pl.BlockSpec(memory_space=pltpu.SMEM)
    return pl.pallas_call(
        kernel,
        out_shape=outs,
        in_specs=[smem] * scalars + [vmem] * n_in,
        out_specs=jax.tree.map(lambda _: vmem, outs),
        compiler_params=pltpu.CompilerParams(vmem_limit_bytes=VMEM_BYTES),
    )


def shape(dims, dtype):
    return jax.ShapeDtypeStruct(dims, dtype)


def local(hidden, in_proj, norm_gain, head_weight, code_ids, stream_mask):
    frames, width = hidden.shape[0], in_proj.shape[1]
    vocab_part = head_weight.shape[1]
    half = frames // 2
    tp = lax.axis_index(TP)
    gain = norm_gain[None, :]
    mine = lax.axis_index("core").reshape(1)
    other = 1 - mine
    code, mask = code_ids[None, :], stream_mask[None, :]
    first_column = (tp * vocab_part).reshape(1)

    steps, inner = 4, hidden.shape[1]
    sent, kept = pl.pallas_call(
        streamed_product,
        out_shape=[shape((half, width), bf16), shape((half, width), f32)],
        in_specs=[pl.BlockSpec(memory_space=pltpu.SMEM)] + [pl.BlockSpec(memory_space=pltpu.HBM)] * 2,
        out_specs=[pl.BlockSpec(memory_space=pltpu.VMEM)] * 2,
        scratch_shapes=[
            pltpu.VMEM((frames, inner), bf16),
            pltpu.VMEM((steps, inner // steps, width), bf16),
            pltpu.SemaphoreType.DMA((steps + 1,)),
        ],
        compiler_params=pltpu.CompilerParams(vmem_limit_bytes=VMEM_BYTES),
    )(mine, *(pltpu.with_memory_space_constraint(array, pltpu.HBM) for array in (hidden, in_proj)))
    chip = in_vmem(chip_sum_of, shape((half, width), bf16), 2, 1)(mine, kept, lax.all_gather(sent, "core"))
    pieces = lax.all_gather(chip, "xl")
    x = add_up(pieces)
    inv_rms = lax.rsqrt(jnp.mean(x * x, axis=1, keepdims=True) + norm_eps)
    unit_rows = x * inv_rms
    normed = lax.all_gather((unit_rows * gain).astype(bf16), "core", tiled=True)

    exp_logits, sums = in_vmem(
        exp_rows, [shape((frames, vocab_part), f32), shape((1, frames), f32)], 2
    )(normed, head_weight)
    totals = lax.all_gather(sums, TP, tiled=True)

    rest = (exp_logits, totals, code, mask, head_weight)
    sent = in_vmem(sent_grad, shape((half, width), bf16), 5, 2)(other, first_column, *rest)
    exp_logits, sent = lax.optimization_barrier((exp_logits, sent))
    rest = (exp_logits, *rest[1:])
    vmem = pl.BlockSpec(memory_space=pltpu.VMEM)
    hbm = pl.BlockSpec(memory_space=pltpu.HBM)
    kept, late_head, early = pl.pallas_call(
        kept_grad,
        out_shape=[
            shape((half, width), f32),
            shape((LATE_BLOCKS - PROJ_BLOCKS, 8, width), bf16),
            shape((4, 96, width), bf16),
        ],
        in_specs=[pl.BlockSpec(memory_space=pltpu.SMEM)] * 2 + [vmem] * 6,
        out_specs=[vmem, vmem, hbm],
        scratch_shapes=[
            pltpu.VMEM((frames, vocab_part), bf16),
            pltpu.VMEM((4, 96, width), bf16),
            pltpu.SemaphoreType.DMA((4,)),
        ],
        compiler_params=pltpu.CompilerParams(vmem_limit_bytes=VMEM_BYTES),
    )(mine, first_column, *rest, normed)
    chip = in_vmem(chip_sum, shape((half, width), bf16), 2)(kept, lax.ppermute(sent, "core", SWAP))
    early, chip = lax.optimization_barrier((early, chip))
    early = lax.all_to_all(early, EARLY, 0, 0)
    own_grad = in_vmem(norm_back, shape((half, width), bf16), 3)(pieces, lax.all_gather(chip, "xl"), gain)
    row_grad = lax.all_gather(own_grad, "core", tiled=True)

    blocks = pl.pallas_call(
        grad_blocks,
        out_shape=shape((N_NEAR, LATE_BLOCKS, width), bf16),
        in_specs=[vmem] * 3,
        out_specs=hbm,
        scratch_shapes=[
            pltpu.VMEM((N_NEAR, LATE_BLOCKS, width), bf16),
            pltpu.SemaphoreType.DMA((N_NEAR,)),
        ],
        compiler_params=pltpu.CompilerParams(vmem_limit_bytes=VMEM_BYTES),
    )(hidden, row_grad, late_head)
    early_out = [shape((48, width), bf16), shape((48, width), f32)]
    early_sent, early_kept = in_vmem(early_sum, early_out, 1, 1)(lax.axis_index("xh").reshape(1), early)
    blocks, early_sent = lax.optimization_barrier((blocks, early_sent))
    pieces = lax.all_to_all(blocks, NEAR, 0, 0)
    early_other = lax.ppermute(early_sent, "xh", SWAP)
    near = in_vmem(near_sum, shape((N_FAR * 8, width), bf16), 3)(
        pieces, early_kept, early_other
    )
    far = lax.all_to_all(near.reshape(N_FAR, 8, width), FAR, 0, 0)
    is_proj = (lax.axis_index(SEQ) < PROJ_BLOCKS).astype(jnp.int32).reshape(1)
    weight_grads = in_vmem(far_sum, shape((16, vocab_part), f32), 1, 1)(is_proj, far)

    hidden_grad = pl.pallas_call(
        hidden_rows,
        out_shape=shape((frames, inner), bf16),
        in_specs=[pl.BlockSpec(memory_space=pltpu.VMEM), pl.BlockSpec(memory_space=pltpu.HBM)],
        out_specs=pl.BlockSpec(memory_space=pltpu.VMEM),
        scratch_shapes=[
            pltpu.VMEM((steps, inner // steps, width), bf16),
            pltpu.SemaphoreType.DMA((steps,)),
        ],
        compiler_params=pltpu.CompilerParams(vmem_limit_bytes=VMEM_BYTES),
        cost_estimate=pl.CostEstimate(
            flops=2 * frames * inner * width, transcendentals=0, bytes_accessed=2 * width * (inner + 2 * frames)
        ),
    )(row_grad, pltpu.with_memory_space_constraint(in_proj, pltpu.HBM))
    return (hidden_grad, weight_grads[None])


def solution(mesh):
    fine = Mesh(mesh.devices.reshape(SIZES), AXES)
    in_specs = (P(SEQ, TP), P(TP, None), P(), P(None, TP), P(SEQ), P(SEQ))
    out_specs = (P(SEQ, TP), P(TP, SEQ, None))
    return jax.shard_map(local, mesh=fine, in_specs=in_specs, out_specs=out_specs, check_vma=False)
```

```python
import jax
import jax.numpy as jnp
from jax import lax
from jax.experimental import pallas as pl
from jax.experimental.pallas import tpu as pltpu
from jax.sharding import Mesh
from jax.sharding import PartitionSpec as P

norm_eps = 1e-05
loss_scale = 16.0

AXES = ("yh", "yl", "xh", "zh", "zl", "xl", "core")
SIZES = (4, 2, 2, 6, 2, 2, 2)
SEQ = ("yh", "yl", "xh", "zh", "zl")
TP = ("xl", "core")
NEAR = ("xh", "yl", "zl")
FAR = ("zh", "yh")
N_NEAR = 8
N_FAR = 24
BLOCKS = 192
PROJ_BLOCKS = 128
LATE_BLOCKS = 144
EARLY = ("yl", "zl")
VMEM_BYTES = 20 << 20
SWAP = [(0, 1), (1, 0)]
f32 = jnp.float32
bf16 = jnp.bfloat16


def dot(a, b, ca, cb):
    return lax.dot_general(a, b, (((ca,), (cb,)), ((), ())), preferred_element_type=f32)


def add_up(pieces):
    total = pieces[0].astype(f32)
    for i in range(1, pieces.shape[0]):
        total = total + pieces[i].astype(f32)
    return total


def place(block):
    y, x, z = block // 24, block // 12 % 2, block % 12
    return y // 2, y % 2, x, z // 2, z % 2


def streamed_product(half_ref, a_hbm, b_hbm, sent_ref, kept_ref, a_ref, b_ref, sems):
    rows, steps, depth = sent_ref.shape[0], b_ref.shape[0], b_ref.shape[1]
    copies = [pltpu.make_async_copy(a_hbm, a_ref, sems.at[steps])]
    for i in range(steps):
        copies.append(pltpu.make_async_copy(b_hbm.at[i * depth : (i + 1) * depth, :], b_ref.at[i], sems.at[i]))
    for copy in copies:
        copy.start()
    copies[0].wait()
    mine = pl.ds(pl.multiple_of(half_ref[0] * rows, rows), rows)
    other = pl.ds(pl.multiple_of((1 - half_ref[0]) * rows, rows), rows)
    sent = kept = None
    for i in range(steps):
        copies[1 + i].wait()
        columns = slice(i * depth, (i + 1) * depth)
        sent_part = dot(a_ref[other, columns], b_ref[i], 1, 0)
        kept_part = dot(a_ref[mine, columns], b_ref[i], 1, 0)
        sent = sent_part if i == 0 else sent + sent_part
        kept = kept_part if i == 0 else kept + kept_part
    sent_ref[...] = sent.astype(sent_ref.dtype)
    kept_ref[...] = kept


def hidden_rows(grad_ref, b_hbm, out_ref, b_ref, sems):
    steps, depth = b_ref.shape[0], b_ref.shape[1]
    copies = [
        pltpu.make_async_copy(b_hbm.at[i * depth : (i + 1) * depth, :], b_ref.at[i], sems.at[i]) for i in range(steps)
    ]
    for copy in copies:
        copy.start()
    for i in range(steps):
        copies[i].wait()
        part = loss_scale * dot(grad_ref[...], b_ref[i], 1, 1)
        out_ref[:, i * depth : (i + 1) * depth] = part.astype(out_ref.dtype)


def exp_rows(normed_ref, head_ref, exp_ref, sum_ref):
    exp_logits = jnp.exp(dot(normed_ref[...], head_ref[...], 1, 0))
    exp_ref[...] = exp_logits
    groups = exp_logits[:, :128]
    for start in range(128, exp_logits.shape[1], 128):
        groups = groups + exp_logits[:, start : start + 128]
    sums = lax.dot_general(
        jnp.ones((8, 128), f32), groups, (((1,), (1,)), ((), ())), precision=lax.Precision.HIGHEST, preferred_element_type=f32
    )
    sum_ref[...] = sums[:1]


def spread(rows):
    ones = jnp.ones((rows.shape[0], 128), f32)
    return lax.dot_general(
        rows, ones, (((0,), (0,)), ((), ())), precision=lax.Precision.HIGHEST, preferred_element_type=f32
    )


def dlogit_rows(first, column, exp_ref, totals_ref, code_ref, mask_ref, rows):
    window = pl.ds(first, rows)
    total, code, weight = (spread(ref[:, window].astype(f32)) for ref in (totals_ref, code_ref, mask_ref))
    scale = weight / total
    parts = []
    for start in range(0, exp_ref.shape[1], 128):
        columns = (lax.broadcasted_iota(jnp.int32, (rows, 128), 1) + (column + start)).astype(f32)
        onehot = jnp.where(columns == code, weight, 0.0)
        parts.append((scale * exp_ref[window, start : start + 128] - onehot).astype(bf16))
    return jnp.concatenate(parts, axis=1)


def sent_grad(half_ref, column_ref, exp_ref, totals_ref, code_ref, mask_ref, head_ref, out_ref):
    rows = out_ref.shape[0]
    start = pl.multiple_of(half_ref[0] * rows, rows)
    dlogit = dlogit_rows(start, column_ref[0], exp_ref, totals_ref, code_ref, mask_ref, rows)
    out_ref[...] = dot(dlogit, head_ref[...], 1, 1).astype(out_ref.dtype)


def copy_out(source_ref, target_hbm, sems):
    copies = [pltpu.make_async_copy(source_ref.at[i], target_hbm.at[i], sems.at[i]) for i in range(source_ref.shape[0])]
    for copy in copies:
        copy.start()
    return copies


def kept_grad(
    half_ref, column_ref, exp_ref, totals_ref, code_ref, mask_ref, head_ref, normed_ref,
    out_ref, late_ref, early_hbm, dlogit_ref, early_ref, sems,
):
    dlogit_ref[...] = dlogit_rows(0, column_ref[0], exp_ref, totals_ref, code_ref, mask_ref, exp_ref.shape[0])
    grad = dot(normed_ref[...], dlogit_ref[...], 0, 0).astype(bf16)
    part = grad.shape[1]
    for i in range(BLOCKS - PROJ_BLOCKS):
        top, bottom = grad[16 * i : 16 * i + 8], grad[16 * i + 8 : 16 * i + 16]
        if PROJ_BLOCKS + i < LATE_BLOCKS:
            late_ref[i, :, :part] = top
            late_ref[i, :, part:] = bottom
        else:
            _, yl, xh, zh, zl = place(PROJ_BLOCKS + i)
            row = 8 * (xh * 6 + zh)
            early_ref[2 * yl + zl, row : row + 8, :part] = top
            early_ref[2 * yl + zl, row : row + 8, part:] = bottom
    copies = copy_out(early_ref, early_hbm, sems)
    rows = out_ref.shape[0]
    start = pl.multiple_of(half_ref[0] * rows, rows)
    out_ref[...] = dot(dlogit_ref[pl.ds(start, rows), :], head_ref[...], 1, 1)
    for copy in copies:
        copy.wait()


def grad_blocks(hidden_ref, grad_ref, head_ref, out_hbm, out_ref, sems):
    step, copies = 16, []
    for first in range(0, LATE_BLOCKS, step):
        if first < PROJ_BLOCKS:
            part = dot(hidden_ref[:, 8 * first : 8 * (first + step)], grad_ref[...], 0, 0).astype(bf16)
        for i in range(step):
            yh, yl, xh, zh, zl = place(first + i)
            row = 8 * (yh * 6 + zh)
            block = part[8 * i : 8 * i + 8] if first < PROJ_BLOCKS else head_ref[i]
            out_ref[(xh * 2 + yl) * 2 + zl, row : row + 8, :] = block
        if (first + step) % 48 == 0:
            done = first // 48
            rows = slice(48 * done, 48 * done + 48)
            for near in range(N_NEAR):
                copies.append(
                    pltpu.make_async_copy(out_ref.at[near, rows], out_hbm.at[near, rows], sems.at[N_NEAR * done + near])
                )
                copies[-1].start()
    for copy in copies:
        copy.wait()


def norm_back(x_ref, grad_ref, gain_ref, out_ref):
    x, grad = add_up(x_ref), add_up(grad_ref)
    inv_rms = lax.rsqrt(jnp.mean(x * x, axis=1, keepdims=True) + norm_eps)
    unit_rows = x * inv_rms
    scaled_grad = grad * gain_ref[...]
    centred = scaled_grad - unit_rows * jnp.mean(scaled_grad * unit_rows, axis=1, keepdims=True)
    out_ref[...] = (inv_rms * centred).astype(out_ref.dtype)


def early_sum(half_ref, pieces_ref, sent_ref, kept_ref):
    rows = sent_ref.shape[0]
    mine = pl.ds(pl.multiple_of(half_ref[0] * rows, rows), rows)
    other = pl.ds(pl.multiple_of((1 - half_ref[0]) * rows, rows), rows)
    sent_ref[...] = add_up(pieces_ref.at[:, other]).astype(sent_ref.dtype)
    kept_ref[...] = add_up(pieces_ref.at[:, mine])


def chip_sum_of(half_ref, kept_ref, both_ref, out_ref):
    out_ref[...] = (kept_ref[...] + both_ref[1 - half_ref[0]].astype(f32)).astype(out_ref.dtype)


def chip_sum(kept_ref, other_ref, out_ref):
    out_ref[...] = (kept_ref[...] + other_ref[...].astype(f32)).astype(out_ref.dtype)


def near_sum(pieces_ref, kept_ref, other_ref, out_ref):
    for zh in range(6):
        for yh in range(3):
            first, row = 8 * (yh * 6 + zh), 8 * (zh * 4 + yh)
            out_ref[row : row + 8] = add_up(pieces_ref.at[:, first : first + 8]).astype(out_ref.dtype)
        window, row = slice(8 * zh, 8 * zh + 8), 8 * (zh * 4 + 3)
        early = kept_ref[window] + other_ref[window].astype(f32)
        out_ref[row : row + 8] = early.astype(out_ref.dtype)


def far_sum(is_proj_ref, pieces_ref, out_ref):
    total = add_up(pieces_ref)
    rows, part = total.shape[0], out_ref.shape[1]

    @pl.when(is_proj_ref[0] == 1)
    def _():
        for row in range(rows):
            out_ref[2 * row : 2 * row + 1, :] = total[row : row + 1, :part]
            out_ref[2 * row + 1 : 2 * row + 2, :] = total[row : row + 1, part:]

    @pl.when(is_proj_ref[0] == 0)
    def _():
        out_ref[:rows, :] = total[:, :part]
        out_ref[rows:, :] = total[:, part:]


def in_vmem(kernel, outs, n_in, scalars=0):
    vmem = pl.BlockSpec(memory_space=pltpu.VMEM)
    smem = pl.BlockSpec(memory_space=pltpu.SMEM)
    return pl.pallas_call(
        kernel,
        out_shape=outs,
        in_specs=[smem] * scalars + [vmem] * n_in,
        out_specs=jax.tree.map(lambda _: vmem, outs),
        compiler_params=pltpu.CompilerParams(vmem_limit_bytes=VMEM_BYTES),
    )


def shape(dims, dtype):
    return jax.ShapeDtypeStruct(dims, dtype)


def local(hidden, in_proj, norm_gain, head_weight, code_ids, stream_mask):
    frames, width = hidden.shape[0], in_proj.shape[1]
    vocab_part = head_weight.shape[1]
    half = frames // 2
    tp = lax.axis_index(TP)
    gain = norm_gain[None, :]
    mine = lax.axis_index("core").reshape(1)
    other = 1 - mine
    code, mask = code_ids[None, :], stream_mask[None, :]
    first_column = (tp * vocab_part).reshape(1)

    steps, inner = 4, hidden.shape[1]
    sent, kept = pl.pallas_call(
        streamed_product,
        out_shape=[shape((half, width), bf16), shape((half, width), f32)],
        in_specs=[pl.BlockSpec(memory_space=pltpu.SMEM)] + [pl.BlockSpec(memory_space=pltpu.HBM)] * 2,
        out_specs=[pl.BlockSpec(memory_space=pltpu.VMEM)] * 2,
        scratch_shapes=[
            pltpu.VMEM((frames, inner), bf16),
            pltpu.VMEM((steps, inner // steps, width), bf16),
            pltpu.SemaphoreType.DMA((steps + 1,)),
        ],
        compiler_params=pltpu.CompilerParams(vmem_limit_bytes=VMEM_BYTES),
    )(mine, *(pltpu.with_memory_space_constraint(array, pltpu.HBM) for array in (hidden, in_proj)))
    chip = in_vmem(chip_sum_of, shape((half, width), bf16), 2, 1)(mine, kept, lax.all_gather(sent, "core"))
    pieces = lax.all_gather(chip, "xl")
    x = add_up(pieces)
    inv_rms = lax.rsqrt(jnp.mean(x * x, axis=1, keepdims=True) + norm_eps)
    unit_rows = x * inv_rms
    normed = lax.all_gather((unit_rows * gain).astype(bf16), "core", tiled=True)

    exp_logits, sums = in_vmem(
        exp_rows, [shape((frames, vocab_part), f32), shape((1, frames), f32)], 2
    )(normed, head_weight)
    totals = lax.all_gather(sums, TP, tiled=True)

    rest = (exp_logits, totals, code, mask, head_weight)
    sent = in_vmem(sent_grad, shape((half, width), bf16), 5, 2)(other, first_column, *rest)
    exp_logits, sent = lax.optimization_barrier((exp_logits, sent))
    rest = (exp_logits, *rest[1:])
    vmem = pl.BlockSpec(memory_space=pltpu.VMEM)
    hbm = pl.BlockSpec(memory_space=pltpu.HBM)
    kept, late_head, early = pl.pallas_call(
        kept_grad,
        out_shape=[
            shape((half, width), f32),
            shape((LATE_BLOCKS - PROJ_BLOCKS, 8, width), bf16),
            shape((4, 96, width), bf16),
        ],
        in_specs=[pl.BlockSpec(memory_space=pltpu.SMEM)] * 2 + [vmem] * 6,
        out_specs=[vmem, vmem, hbm],
        scratch_shapes=[
            pltpu.VMEM((frames, vocab_part), bf16),
            pltpu.VMEM((4, 96, width), bf16),
            pltpu.SemaphoreType.DMA((4,)),
        ],
        compiler_params=pltpu.CompilerParams(vmem_limit_bytes=VMEM_BYTES),
    )(mine, first_column, *rest, normed)
    chip = in_vmem(chip_sum, shape((half, width), bf16), 2)(kept, lax.ppermute(sent, "core", SWAP))
    early, chip = lax.optimization_barrier((early, chip))
    early = lax.all_to_all(early, EARLY, 0, 0)
    own_grad = in_vmem(norm_back, shape((half, width), bf16), 3)(pieces, lax.all_gather(chip, "xl"), gain)
    row_grad = lax.all_gather(own_grad, "core", tiled=True)

    blocks = pl.pallas_call(
        grad_blocks,
        out_shape=shape((N_NEAR, LATE_BLOCKS, width), bf16),
        in_specs=[vmem] * 3,
        out_specs=hbm,
        scratch_shapes=[
            pltpu.VMEM((N_NEAR, LATE_BLOCKS, width), bf16),
            pltpu.SemaphoreType.DMA((3 * N_NEAR,)),
        ],
        compiler_params=pltpu.CompilerParams(vmem_limit_bytes=VMEM_BYTES),
    )(hidden, row_grad, late_head)
    early_out = [shape((48, width), bf16), shape((48, width), f32)]
    early_sent, early_kept = in_vmem(early_sum, early_out, 1, 1)(lax.axis_index("xh").reshape(1), early)
    blocks, early_sent = lax.optimization_barrier((blocks, early_sent))
    pieces = lax.all_to_all(blocks, NEAR, 0, 0)
    early_other = lax.ppermute(early_sent, "xh", SWAP)
    near = in_vmem(near_sum, shape((N_FAR * 8, width), bf16), 3)(
        pieces, early_kept, early_other
    )
    far = lax.all_to_all(near.reshape(N_FAR, 8, width), FAR, 0, 0)
    is_proj = (lax.axis_index(SEQ) < PROJ_BLOCKS).astype(jnp.int32).reshape(1)
    weight_grads = in_vmem(far_sum, shape((16, vocab_part), f32), 1, 1)(is_proj, far)

    hidden_grad = pl.pallas_call(
        hidden_rows,
        out_shape=shape((frames, inner), bf16),
        in_specs=[pl.BlockSpec(memory_space=pltpu.VMEM), pl.BlockSpec(memory_space=pltpu.HBM)],
        out_specs=pl.BlockSpec(memory_space=pltpu.VMEM),
        scratch_shapes=[
            pltpu.VMEM((steps, inner // steps, width), bf16),
            pltpu.SemaphoreType.DMA((steps,)),
        ],
        compiler_params=pltpu.CompilerParams(vmem_limit_bytes=VMEM_BYTES),
        cost_estimate=pl.CostEstimate(
            flops=2 * frames * inner * width, transcendentals=0, bytes_accessed=2 * width * (inner + 2 * frames)
        ),
    )(row_grad, pltpu.with_memory_space_constraint(in_proj, pltpu.HBM))
    return (hidden_grad, weight_grads[None])


def solution(mesh):
    fine = Mesh(mesh.devices.reshape(SIZES), AXES)
    in_specs = (P(SEQ, TP), P(TP, None), P(), P(None, TP), P(SEQ), P(SEQ))
    out_specs = (P(SEQ, TP), P(TP, SEQ, None))
    return jax.shard_map(local, mesh=fine, in_specs=in_specs, out_specs=out_specs, check_vma=False)
```

```python
import jax
import jax.numpy as jnp
from jax import lax
from jax.experimental import pallas as pl
from jax.experimental.pallas import tpu as pltpu
from jax.sharding import Mesh
from jax.sharding import PartitionSpec as P

norm_eps = 1e-05
loss_scale = 16.0

AXES = ("yh", "yl", "xh", "zh", "zl", "xl", "core")
SIZES = (4, 2, 2, 6, 2, 2, 2)
SEQ = ("yh", "yl", "xh", "zh", "zl")
TP = ("xl", "core")
NEAR = ("xh", "yl", "zl")
FAR = ("zh", "yh")
N_NEAR = 8
N_FAR = 24
BLOCKS = 192
PROJ_BLOCKS = 128
LATE_BLOCKS = 144
EARLY = ("yl", "zl")
VMEM_BYTES = 20 << 20
SWAP = [(0, 1), (1, 0)]
f32 = jnp.float32
bf16 = jnp.bfloat16


def dot(a, b, ca, cb):
    return lax.dot_general(a, b, (((ca,), (cb,)), ((), ())), preferred_element_type=f32)


def add_up(pieces):
    total = pieces[0].astype(f32)
    for i in range(1, pieces.shape[0]):
        total = total + pieces[i].astype(f32)
    return total


def place(block):
    y, x, z = block // 24, block // 12 % 2, block % 12
    return y // 2, y % 2, x, z // 2, z % 2


def streamed_product(half_ref, a_hbm, b_hbm, sent_ref, kept_ref, a_ref, b_ref, sems):
    rows, steps, depth = sent_ref.shape[0], b_ref.shape[0], b_ref.shape[1]
    copies = [pltpu.make_async_copy(a_hbm, a_ref, sems.at[steps])]
    for i in range(steps):
        copies.append(pltpu.make_async_copy(b_hbm.at[i * depth : (i + 1) * depth, :], b_ref.at[i], sems.at[i]))
    for copy in copies:
        copy.start()
    copies[0].wait()
    mine = pl.ds(pl.multiple_of(half_ref[0] * rows, rows), rows)
    other = pl.ds(pl.multiple_of((1 - half_ref[0]) * rows, rows), rows)
    sent = kept = None
    for i in range(steps):
        copies[1 + i].wait()
        columns = slice(i * depth, (i + 1) * depth)
        sent_part = dot(a_ref[other, columns], b_ref[i], 1, 0)
        kept_part = dot(a_ref[mine, columns], b_ref[i], 1, 0)
        sent = sent_part if i == 0 else sent + sent_part
        kept = kept_part if i == 0 else kept + kept_part
    sent_ref[...] = sent.astype(sent_ref.dtype)
    kept_ref[...] = kept


def hidden_rows(grad_ref, b_hbm, out_ref, b_ref, sems):
    steps, depth = b_ref.shape[0], b_ref.shape[1]
    copies = [
        pltpu.make_async_copy(b_hbm.at[i * depth : (i + 1) * depth, :], b_ref.at[i], sems.at[i]) for i in range(steps)
    ]
    for copy in copies:
        copy.start()
    for i in range(steps):
        copies[i].wait()
        part = loss_scale * dot(grad_ref[...], b_ref[i], 1, 1)
        out_ref[:, i * depth : (i + 1) * depth] = part.astype(out_ref.dtype)


def exp_rows(normed_ref, head_ref, exp_ref, sum_ref):
    exp_logits = jnp.exp(dot(normed_ref[...], head_ref[...], 1, 0))
    exp_ref[...] = exp_logits
    groups = exp_logits[:, :128]
    for start in range(128, exp_logits.shape[1], 128):
        groups = groups + exp_logits[:, start : start + 128]
    sums = lax.dot_general(
        jnp.ones((8, 128), f32), groups, (((1,), (1,)), ((), ())), precision=lax.Precision.HIGHEST, preferred_element_type=f32
    )
    sum_ref[...] = sums[:1]


def spread(rows):
    ones = jnp.ones((rows.shape[0], 128), f32)
    return lax.dot_general(
        rows, ones, (((0,), (0,)), ((), ())), precision=lax.Precision.HIGHEST, preferred_element_type=f32
    )


def dlogit_rows(first, column, exp_ref, totals_ref, code_ref, mask_ref, rows):
    window = pl.ds(first, rows)
    total, code, weight = (spread(ref[:, window].astype(f32)) for ref in (totals_ref, code_ref, mask_ref))
    scale = weight / total
    parts = []
    for start in range(0, exp_ref.shape[1], 128):
        columns = (lax.broadcasted_iota(jnp.int32, (rows, 128), 1) + (column + start)).astype(f32)
        onehot = jnp.where(columns == code, weight, 0.0)
        parts.append((scale * exp_ref[window, start : start + 128] - onehot).astype(bf16))
    return jnp.concatenate(parts, axis=1)


def sent_grad(half_ref, column_ref, exp_ref, totals_ref, code_ref, mask_ref, head_ref, out_ref):
    rows = out_ref.shape[0]
    start = pl.multiple_of(half_ref[0] * rows, rows)
    dlogit = dlogit_rows(start, column_ref[0], exp_ref, totals_ref, code_ref, mask_ref, rows)
    out_ref[...] = dot(dlogit, head_ref[...], 1, 1).astype(out_ref.dtype)


def copy_out(source_ref, target_hbm, sems):
    copies = [pltpu.make_async_copy(source_ref.at[i], target_hbm.at[i], sems.at[i]) for i in range(source_ref.shape[0])]
    for copy in copies:
        copy.start()
    return copies


def kept_grad(
    half_ref, column_ref, exp_ref, totals_ref, code_ref, mask_ref, head_ref, normed_ref,
    out_ref, late_ref, early_hbm, dlogit_ref, early_ref, sems,
):
    dlogit_ref[...] = dlogit_rows(0, column_ref[0], exp_ref, totals_ref, code_ref, mask_ref, exp_ref.shape[0])
    grad = dot(normed_ref[...], dlogit_ref[...], 0, 0).astype(bf16)
    part = grad.shape[1]
    for i in range(BLOCKS - PROJ_BLOCKS):
        top, bottom = grad[16 * i : 16 * i + 8], grad[16 * i + 8 : 16 * i + 16]
        if PROJ_BLOCKS + i < LATE_BLOCKS:
            late_ref[i, :, :part] = top
            late_ref[i, :, part:] = bottom
        else:
            _, yl, xh, zh, zl = place(PROJ_BLOCKS + i)
            row = 8 * (xh * 6 + zh)
            early_ref[2 * yl + zl, row : row + 8, :part] = top
            early_ref[2 * yl + zl, row : row + 8, part:] = bottom
    copies = copy_out(early_ref, early_hbm, sems)
    rows = out_ref.shape[0]
    start = pl.multiple_of(half_ref[0] * rows, rows)
    out_ref[...] = dot(dlogit_ref[pl.ds(start, rows), :], head_ref[...], 1, 1)
    for copy in copies:
        copy.wait()


def grad_blocks(hidden_ref, grad_ref, head_ref, out_hbm, out_ref, sems):
    step, copies = 16, []
    for first in range(0, LATE_BLOCKS, step):
        if first < PROJ_BLOCKS:
            part = dot(hidden_ref[:, 8 * first : 8 * (first + step)], grad_ref[...], 0, 0).astype(bf16)
        for i in range(step):
            yh, yl, xh, zh, zl = place(first + i)
            row = 8 * (yh * 6 + zh)
            block = part[8 * i : 8 * i + 8] if first < PROJ_BLOCKS else head_ref[i]
            out_ref[(xh * 2 + yl) * 2 + zl, row : row + 8, :] = block
        if (first + step) % 48 == 0:
            done = first // 48
            rows = slice(48 * done, 48 * done + 48)
            for near in range(N_NEAR):
                copies.append(
                    pltpu.make_async_copy(out_ref.at[near, rows], out_hbm.at[near, rows], sems.at[N_NEAR * done + near])
                )
                copies[-1].start()
    for copy in copies:
        copy.wait()


def norm_back(x_ref, grad_ref, gain_ref, out_ref):
    x, grad = add_up(x_ref), add_up(grad_ref)
    inv_rms = lax.rsqrt(jnp.mean(x * x, axis=1, keepdims=True) + norm_eps)
    unit_rows = x * inv_rms
    scaled_grad = grad * gain_ref[...]
    centred = scaled_grad - unit_rows * jnp.mean(scaled_grad * unit_rows, axis=1, keepdims=True)
    out_ref[...] = (inv_rms * centred).astype(out_ref.dtype)


def early_sum(half_ref, pieces_ref, sent_ref, kept_ref):
    rows = sent_ref.shape[0]
    mine = pl.ds(pl.multiple_of(half_ref[0] * rows, rows), rows)
    other = pl.ds(pl.multiple_of((1 - half_ref[0]) * rows, rows), rows)
    sent_ref[...] = add_up(pieces_ref.at[:, other]).astype(sent_ref.dtype)
    kept_ref[...] = add_up(pieces_ref.at[:, mine])


def chip_sum_of(half_ref, kept_ref, both_ref, out_ref):
    out_ref[...] = (kept_ref[...] + both_ref[1 - half_ref[0]].astype(f32)).astype(out_ref.dtype)


def chip_sum(kept_ref, other_ref, out_ref):
    out_ref[...] = (kept_ref[...] + other_ref[...].astype(f32)).astype(out_ref.dtype)


def near_sum(pieces_ref, kept_ref, other_ref, out_ref):
    for zh in range(6):
        for yh in range(3):
            first, row = 8 * (yh * 6 + zh), 8 * (zh * 4 + yh)
            out_ref[row : row + 8] = add_up(pieces_ref.at[:, first : first + 8]).astype(out_ref.dtype)
        window, row = slice(8 * zh, 8 * zh + 8), 8 * (zh * 4 + 3)
        early = kept_ref[window] + other_ref[window].astype(f32)
        out_ref[row : row + 8] = early.astype(out_ref.dtype)


def far_sum(is_proj_ref, pieces_ref, out_ref):
    total = add_up(pieces_ref)
    rows, part = total.shape[0], out_ref.shape[1]

    @pl.when(is_proj_ref[0] == 1)
    def _():
        for row in range(rows):
            out_ref[2 * row : 2 * row + 1, :] = total[row : row + 1, :part]
            out_ref[2 * row + 1 : 2 * row + 2, :] = total[row : row + 1, part:]

    @pl.when(is_proj_ref[0] == 0)
    def _():
        out_ref[:rows, :] = total[:, :part]
        out_ref[rows:, :] = total[:, part:]


def in_vmem(kernel, outs, n_in, scalars=0):
    vmem = pl.BlockSpec(memory_space=pltpu.VMEM)
    smem = pl.BlockSpec(memory_space=pltpu.SMEM)
    return pl.pallas_call(
        kernel,
        out_shape=outs,
        in_specs=[smem] * scalars + [vmem] * n_in,
        out_specs=jax.tree.map(lambda _: vmem, outs),
        compiler_params=pltpu.CompilerParams(vmem_limit_bytes=VMEM_BYTES),
    )


def shape(dims, dtype):
    return jax.ShapeDtypeStruct(dims, dtype)


def local(hidden, in_proj, norm_gain, head_weight, code_ids, stream_mask):
    frames, width = hidden.shape[0], in_proj.shape[1]
    vocab_part = head_weight.shape[1]
    half = frames // 2
    tp = lax.axis_index(TP)
    gain = norm_gain[None, :]
    mine = lax.axis_index("core").reshape(1)
    other = 1 - mine
    code, mask = code_ids[None, :], stream_mask[None, :]
    first_column = (tp * vocab_part).reshape(1)

    steps, inner = 2, hidden.shape[1]
    sent, kept = pl.pallas_call(
        streamed_product,
        out_shape=[shape((half, width), bf16), shape((half, width), f32)],
        in_specs=[pl.BlockSpec(memory_space=pltpu.SMEM)] + [pl.BlockSpec(memory_space=pltpu.HBM)] * 2,
        out_specs=[pl.BlockSpec(memory_space=pltpu.VMEM)] * 2,
        scratch_shapes=[
            pltpu.VMEM((frames, inner), bf16),
            pltpu.VMEM((steps, inner // steps, width), bf16),
            pltpu.SemaphoreType.DMA((steps + 1,)),
        ],
        compiler_params=pltpu.CompilerParams(vmem_limit_bytes=VMEM_BYTES),
    )(mine, *(pltpu.with_memory_space_constraint(array, pltpu.HBM) for array in (hidden, in_proj)))
    chip = in_vmem(chip_sum_of, shape((half, width), bf16), 2, 1)(mine, kept, lax.all_gather(sent, "core"))
    pieces = lax.all_gather(chip, "xl")
    x = add_up(pieces)
    inv_rms = lax.rsqrt(jnp.mean(x * x, axis=1, keepdims=True) + norm_eps)
    unit_rows = x * inv_rms
    normed = lax.all_gather((unit_rows * gain).astype(bf16), "core", tiled=True)

    exp_logits, sums = in_vmem(
        exp_rows, [shape((frames, vocab_part), f32), shape((1, frames), f32)], 2
    )(normed, head_weight)
    totals = lax.all_gather(sums, TP, tiled=True)

    rest = (exp_logits, totals, code, mask, head_weight)
    sent = in_vmem(sent_grad, shape((half, width), bf16), 5, 2)(other, first_column, *rest)
    exp_logits, sent = lax.optimization_barrier((exp_logits, sent))
    rest = (exp_logits, *rest[1:])
    vmem = pl.BlockSpec(memory_space=pltpu.VMEM)
    hbm = pl.BlockSpec(memory_space=pltpu.HBM)
    kept, late_head, early = pl.pallas_call(
        kept_grad,
        out_shape=[
            shape((half, width), f32),
            shape((LATE_BLOCKS - PROJ_BLOCKS, 8, width), bf16),
            shape((4, 96, width), bf16),
        ],
        in_specs=[pl.BlockSpec(memory_space=pltpu.SMEM)] * 2 + [vmem] * 6,
        out_specs=[vmem, vmem, hbm],
        scratch_shapes=[
            pltpu.VMEM((frames, vocab_part), bf16),
            pltpu.VMEM((4, 96, width), bf16),
            pltpu.SemaphoreType.DMA((4,)),
        ],
        compiler_params=pltpu.CompilerParams(vmem_limit_bytes=VMEM_BYTES),
    )(mine, first_column, *rest, normed)
    chip = in_vmem(chip_sum, shape((half, width), bf16), 2)(kept, lax.ppermute(sent, "core", SWAP))
    early, chip = lax.optimization_barrier((early, chip))
    early = lax.all_to_all(early, EARLY, 0, 0)
    own_grad = in_vmem(norm_back, shape((half, width), bf16), 3)(pieces, lax.all_gather(chip, "xl"), gain)
    row_grad = lax.all_gather(own_grad, "core", tiled=True)

    blocks = pl.pallas_call(
        grad_blocks,
        out_shape=shape((N_NEAR, LATE_BLOCKS, width), bf16),
        in_specs=[vmem] * 3,
        out_specs=hbm,
        scratch_shapes=[
            pltpu.VMEM((N_NEAR, LATE_BLOCKS, width), bf16),
            pltpu.SemaphoreType.DMA((3 * N_NEAR,)),
        ],
        compiler_params=pltpu.CompilerParams(vmem_limit_bytes=VMEM_BYTES),
    )(hidden, row_grad, late_head)
    early_out = [shape((48, width), bf16), shape((48, width), f32)]
    early_sent, early_kept = in_vmem(early_sum, early_out, 1, 1)(lax.axis_index("xh").reshape(1), early)
    blocks, early_sent = lax.optimization_barrier((blocks, early_sent))
    pieces = lax.all_to_all(blocks, NEAR, 0, 0)
    early_other = lax.ppermute(early_sent, "xh", SWAP)
    near = in_vmem(near_sum, shape((N_FAR * 8, width), bf16), 3)(
        pieces, early_kept, early_other
    )
    far = lax.all_to_all(near.reshape(N_FAR, 8, width), FAR, 0, 0)
    is_proj = (lax.axis_index(SEQ) < PROJ_BLOCKS).astype(jnp.int32).reshape(1)
    weight_grads = in_vmem(far_sum, shape((16, vocab_part), f32), 1, 1)(is_proj, far)

    hidden_grad = pl.pallas_call(
        hidden_rows,
        out_shape=shape((frames, inner), bf16),
        in_specs=[pl.BlockSpec(memory_space=pltpu.VMEM), pl.BlockSpec(memory_space=pltpu.HBM)],
        out_specs=pl.BlockSpec(memory_space=pltpu.VMEM),
        scratch_shapes=[
            pltpu.VMEM((steps, inner // steps, width), bf16),
            pltpu.SemaphoreType.DMA((steps,)),
        ],
        compiler_params=pltpu.CompilerParams(vmem_limit_bytes=VMEM_BYTES),
        cost_estimate=pl.CostEstimate(
            flops=2 * frames * inner * width, transcendentals=0, bytes_accessed=2 * width * (inner + 2 * frames)
        ),
    )(row_grad, pltpu.with_memory_space_constraint(in_proj, pltpu.HBM))
    return (hidden_grad, weight_grads[None])


def solution(mesh):
    fine = Mesh(mesh.devices.reshape(SIZES), AXES)
    in_specs = (P(SEQ, TP), P(TP, None), P(), P(None, TP), P(SEQ), P(SEQ))
    out_specs = (P(SEQ, TP), P(TP, SEQ, None))
    return jax.shard_map(local, mesh=fine, in_specs=in_specs, out_specs=out_specs, check_vma=False)
```
